256 devices in a mesh: wide: 32 (over z, y), qa: 4 (over x), qb: 2 (over core).
Axes of the slice: x: 4, y: 4, z: 8, core: 2. Of those that a mesh axis runs over, the one named last changes fastest.
Arguments:
- core_slices: float32 [262144, 256], P(('wide', 'qa', 'qb')), may hold values from -64 to 64
- next_core: float32 [256, 16384], P('wide', ('qa', 'qb')), may hold values from -0.375 to 0.375
Outputs:
- ortho_basis: float32 [262144, 256], P(('wide', 'qa', 'qb'))
- new_core: float32 [256, 16384], P('wide', ('qa', 'qb'))
The draws below stay inside these ranges and needn't reach their ends.
All inputs are finite; a program needn't handle non-finite values.
Results may differ from the reference program's by a relative error of at most 0.0003.
Values sent between devices are 32-bit elements; how exact they have to be, the bound alone decides.
No kernel may reach another device: no remote copies, remote signals or barrier semaphores. Data moves between devices by JAX's collectives and lax.ppermute only.
A program may use at most 128 MiB of HBM per device.

```python
import jax
import jax.numpy as jnp
from jax import lax

RANK = 256
ROWS_DEV = 1024
NEXT_COLS = 16384
ROWS = 262144


def draw_core_slices(key, part):
    keys = jax.random.split(jax.random.fold_in(key, 7), 4)
    block_rows = min(256, ROWS_DEV)
    blocks = ROWS // block_rows
    row_scale = jnp.repeat(10.0 ** jax.random.uniform(keys[0], (blocks, 1), jnp.float32), block_rows, axis=0)
    rank_order = jax.random.permutation(keys[1], RANK).astype(jnp.float32)
    spread = 10.0 ** (-2.75 * rank_order / (RANK - 1))
    positions = jnp.arange(RANK, dtype=jnp.float32)
    cosine = jnp.sqrt(2.0 / RANK) * jnp.cos(jnp.pi * (2.0 * positions[None, :] + 1.0) * positions[:, None] / (2.0 * RANK))
    cosine = cosine * jnp.where(positions[:, None] == 0.0, jnp.sqrt(0.5), 1.0)
    sign_flips = jnp.where(jax.random.bernoulli(keys[2], 0.5, (1, RANK)), 1.0, -1.0)
    mixing = spread[:, None] * cosine * sign_flips
    values = jnp.clip(jax.random.normal(keys[3], (ROWS, RANK), jnp.float32), -4.0, 4.0)
    mixed_rows = jnp.dot(values, mixing, precision=lax.Precision.HIGHEST, preferred_element_type=jnp.float32)
    return jnp.clip(mixed_rows * row_scale, -64.0, 64.0).astype(jnp.float32)


def block_scale(key, shape, cuts, low, largest):
    def one(dim, parts):
        steps = jax.random.uniform(jax.random.fold_in(jax.random.fold_in(key, 6), dim), (parts,), jnp.float32, low / len(cuts), largest / len(cuts))
        return jnp.repeat(jnp.exp(steps), shape[dim] // parts).reshape((-1,) + (1,) * (len(shape) - dim - 1))

    gain = one(*cuts[0])
    for cut in cuts[1:]:
        gain = gain * one(*cut)
    return gain


def gaussian(stream_key, extent, scale, bound, cuts=(), kind=jnp.bfloat16):
    array = scale * jax.random.normal(stream_key, extent, jnp.float32)
    if cuts:
        array = array * block_scale(stream_key, extent, cuts, -0.22, 0.18)
    return jnp.clip(array, -bound, bound).astype(kind)


def setup_inputs(seed: int = 0) -> dict:
    streams_of = jax.random.split(jax.random.key(seed), 3)
    return {
        "core_slices": draw_core_slices(jax.random.fold_in(streams_of[2], 71), 0),
        "next_core": gaussian(streams_of[1], (RANK, NEXT_COLS), RANK ** -0.5, 0.375, ((0, 32), (1, 8)), jnp.float32),
    }


def leaf_parts(gram):
    count = gram.shape[0]
    places = jnp.arange(count)
    work = gram
    lower = jnp.zeros_like(gram)
    for k in range(count):
        column = work[:, k]
        column = jnp.where(places >= k, column / jnp.sqrt(column[k]), jnp.zeros_like(column))
        work = work - column[:, None] * column[None, :]
        lower = lower.at[:, k].set(column)
    inverse = jnp.zeros_like(gram)
    for k in range(count):
        row = lower[k]
        earlier = jnp.where(places < k, row, jnp.zeros_like(row))
        unit = jnp.where(places == k, jnp.ones_like(row), jnp.zeros_like(row))
        carried = jnp.dot(earlier, inverse, precision=lax.Precision.HIGHEST, preferred_element_type=gram.dtype)
        inverse = inverse.at[k].set((unit - carried) / row[k])
    return (lower, inverse)

def lower_parts(gram):
    count = gram.shape[0]
    if count <= 16:
        return leaf_parts(gram)
    half = count // 2
    lower_top, inverse_top = lower_parts(gram[:half, :half])
    lower_side = jnp.dot(gram[half:, :half], inverse_top.T, precision=lax.Precision.HIGHEST, preferred_element_type=gram.dtype)
    schur = gram[half:, half:] - jnp.dot(lower_side, lower_side.T, precision=lax.Precision.HIGHEST, preferred_element_type=gram.dtype)
    lower_end, inverse_end = lower_parts(schur)
    inverse_side = -jnp.dot(jnp.dot(inverse_end, lower_side, precision=lax.Precision.HIGHEST, preferred_element_type=gram.dtype), inverse_top, precision=lax.Precision.HIGHEST, preferred_element_type=gram.dtype)
    zeros_block = jnp.zeros((half, count - half), gram.dtype)
    lower = jnp.concatenate([jnp.concatenate([lower_top, zeros_block], axis=1), jnp.concatenate([lower_side, lower_end], axis=1)], axis=0)
    inverse = jnp.concatenate([jnp.concatenate([inverse_top, zeros_block], axis=1), jnp.concatenate([inverse_side, inverse_end], axis=1)], axis=0)
    return (lower, inverse)

def upper_factor(gram):
    lower, inverse_lower = lower_parts(gram)
    return (lower.T, inverse_lower.T)

def reference(core_slices, next_core):
    halved = core_slices.astype(jnp.bfloat16)
    first_gram = lax.dot_general(halved, halved, (((0,), (0,)), ((), ())), preferred_element_type=jnp.float32) / ROWS
    upper_one, inverse_one = upper_factor(first_gram)
    section_one = jnp.dot(core_slices, inverse_one, precision=lax.Precision.HIGHEST, preferred_element_type=jnp.float32)
    second_gram = lax.dot_general(section_one, section_one, (((0,), (0,)), ((), ())), precision=lax.Precision.HIGHEST, preferred_element_type=jnp.float32) / ROWS
    upper_two, inverse_two = upper_factor(second_gram)
    ortho_basis = jnp.dot(section_one, inverse_two, precision=lax.Precision.HIGHEST, preferred_element_type=jnp.float32)
    factor = jnp.dot(upper_two, upper_one, precision=lax.Precision.HIGHEST, preferred_element_type=jnp.float32)
    new_core = jnp.dot(factor, next_core, precision=lax.Precision.HIGHEST, preferred_element_type=jnp.float32)
    return (ortho_basis, new_core)
```

```python
import functools

import jax
import jax.numpy as jnp
from jax import lax
from jax.experimental import pallas as pl
from jax.experimental.pallas import tpu as pltpu
from jax.sharding import PartitionSpec as P


HALF = 128
SUB = 8
F32 = jnp.float32
NT = (((1,), (1,)), ((), ()))
NN = (((1,), (0,)), ((), ()))
TN = (((0,), (0,)), ((), ()))


def mul(a, b, dims):
    return lax.dot_general(
        a, b, dims, precision=lax.Precision.HIGHEST, preferred_element_type=F32
    )


def row_of(x, j):
    return jnp.broadcast_to(x[j : j + 1, :], x.shape)


def column_of(x, k):
    return jnp.broadcast_to(x[:, k : k + 1], x.shape)


def eliminate(work_ref, upper_ref, inverse_ref, at):
    groups = HALF // SUB
    lane = lax.broadcasted_iota(jnp.int32, (SUB, HALF), 1)
    place = lax.broadcasted_iota(jnp.int32, (SUB, HALF), 0)
    zero = jnp.zeros((SUB, HALF), F32)
    for b in range(groups):
        first = b * SUB
        inside = (lane >= first) & (lane < first + SUB)
        own = work_ref[first : first + SUB, :]
        columns = [column_of(own, first + j) for j in range(SUB)]
        rows = jnp.where(inside, jnp.where(lane - first == place, 1.0, 0.0), own)
        inverses, across, pivots, pivot_rows = [], [], [], []
        for j in range(SUB):
            pivot = row_of(columns[j], j)
            inverse = 1.0 / pivot
            ratio = jnp.where(place > j, columns[j] * inverse, zero)
            ahead = {}
            for i in range(j + 1, SUB):
                ahead[i] = row_of(columns[i], j)
                columns[i] = columns[i] - ratio * ahead[i]
            pivot_row = row_of(rows, j)
            rows = rows - ratio * pivot_row
            inverses.append(inverse)
            across.append(ahead)
            pivots.append(pivot)
            pivot_rows.append(pivot_row)
        for g in range(b + 1, groups):
            other = work_ref[g * SUB : (g + 1) * SUB, :]
            parts = [column_of(other, first + j) for j in range(SUB)]
            other = jnp.where(inside, zero, other)
            for j in range(SUB):
                ratio = parts[j] * inverses[j]
                for i in range(j + 1, SUB):
                    parts[i] = parts[i] - ratio * across[j][i]
                other = other - ratio * pivot_rows[j]
            work_ref[g * SUB : (g + 1) * SUB, :] = other
        pivot_column = pivots[0]
        for j in range(1, SUB):
            pivot_column = jnp.where(place == j, pivots[j], pivot_column)
        root = jnp.sqrt(pivot_column)
        scale = 1.0 / root
        rows = rows * scale
        upper = jnp.where(lane >= first + SUB, rows, zero)
        for j in range(SUB):
            upper = jnp.where((lane == first + j) & (place <= j), columns[j] * scale, upper)
        upper_ref[at + first : at + first + SUB, at : at + HALF] = upper
        inverse_ref[at + first : at + first + SUB, at : at + HALF] = jnp.where(
            lane < first + SUB, rows, zero
        )


def factor_gram(gram_ref, scale, work_ref, upper_ref, inverse_ref):
    work_ref[...] = gram_ref[0:HALF, :] * scale
    eliminate(work_ref, upper_ref, inverse_ref, 0)
    side = gram_ref[HALF : 2 * HALF, :] * scale
    inverse_top = inverse_ref[0:HALF, 0:HALF]
    upper_side = mul(inverse_top, side, NN)
    upper_ref[0:HALF, HALF:] = upper_side
    upper_ref[HALF:, 0:HALF] = jnp.zeros((HALF, HALF), F32)
    work_ref[...] = gram_ref[2 * HALF :, :] * scale - mul(upper_side, upper_side, TN)
    carried = mul(upper_side, inverse_top, TN)
    eliminate(work_ref, upper_ref, inverse_ref, HALF)
    inverse_ref[HALF:, 0:HALF] = -mul(inverse_ref[HALF:, HALF:], carried, NN)
    inverse_ref[0:HALF, HALF:] = jnp.zeros((HALF, HALF), F32)


CHUNK = 256


def first_kernel(scale, gram_ref, core_ref, section_ref, upper_ref, second_ref, work_ref, inverse_ref):
    factor_gram(gram_ref, scale, work_ref, upper_ref, inverse_ref)
    second_ref[...] = jnp.zeros_like(second_ref)

    @pl.loop(0, core_ref.shape[0] // CHUNK)
    def _(step):
        here = pl.ds(pl.multiple_of(step * CHUNK, CHUNK), CHUNK)
        section = mul(core_ref[here, :], inverse_ref[...], NT)
        section_ref[here, :] = section
        gram = mul(section, section, TN)
        second_ref[0:HALF, :] += gram[0:HALF, 0:HALF]
        second_ref[HALF : 2 * HALF, :] += gram[0:HALF, HALF:]
        second_ref[2 * HALF :, :] += gram[HALF:, HALF:]


def second_kernel(
    scale, gram_ref, section_ref, first_ref, ortho_ref, factor_ref, work_ref, upper_ref, inverse_ref
):
    factor_gram(gram_ref, scale, work_ref, upper_ref, inverse_ref)
    factor_ref[...] = mul(upper_ref[...], first_ref[...], NN)

    @pl.loop(0, section_ref.shape[0] // CHUNK)
    def _(step):
        here = pl.ds(pl.multiple_of(step * CHUNK, CHUNK), CHUNK)
        ortho_ref[here, :] = mul(section_ref[here, :], inverse_ref[...], NT)


def exchange(value, axis, pairs):
    return lax.ppermute(value, axis, pairs)


def shifted(value, axis, place_of):
    return exchange(value, axis, [(place_of(i), i) for i in range(lax.axis_size(axis))])


def gram_total(blocks, depth):
    half = blocks.shape[0] // 2
    low = lax.axis_index("qb") == 0
    mine = jnp.where(low, blocks[:half], blocks[half:])
    mine = mine + shifted(jnp.where(low, blocks[half:], blocks[:half]), "qb", lambda i: 1 - i)

    def around(value, axis, place):
        one, two, three = (shifted(value, axis, functools.partial(place, d)) for d in (1, 2, 3))
        return (value + two) + (one + three)

    long = lax.axis_size("wide") // depth
    mine = around(mine, "qa", lambda d, i: (i + d) % 4)
    mine = around(mine, "wide", lambda d, i: i // depth * depth + (i + d) % depth)
    mine = mine + shifted(mine, "wide", lambda i: (i // depth + 4) % long * depth + i % depth)
    mine = around(mine, "wide", lambda d, i: (i // depth + (1, 2, -1)[d - 1]) % long * depth + i % depth)
    other = shifted(mine, "qb", lambda i: 1 - i)
    return jnp.where(
        low, jnp.concatenate([mine, other], axis=0), jnp.concatenate([other, mine], axis=0)
    )


def per_device(core_slices, next_core):
    rows, rank = core_slices.shape
    total_rows = rows * lax.axis_size("wide") * lax.axis_size("qa") * lax.axis_size("qb")
    depth = 4
    whole_next = lax.all_gather(next_core, "wide", axis=0, tiled=True)
    halved = core_slices.astype(jnp.bfloat16)
    local = lax.dot_general(halved, halved, TN, preferred_element_type=F32)
    blocks = jnp.concatenate([local[:HALF, :HALF], local[:HALF, HALF:], local[HALF:, HALF:]], axis=0)
    blocks = gram_total(blocks, depth)
    square = jax.ShapeDtypeStruct((rank, rank), F32)
    tall = jax.ShapeDtypeStruct((rows, rank), F32)
    vmem = pl.BlockSpec(memory_space=pltpu.VMEM)
    scratch = [pltpu.VMEM((HALF, HALF), F32), pltpu.VMEM((rank, rank), F32)]
    section, upper_one, second = pl.pallas_call(
        functools.partial(first_kernel, 1.0 / total_rows),
        out_shape=(tall, square, jax.ShapeDtypeStruct((3 * HALF, HALF), F32)),
        in_specs=[vmem] * 2,
        out_specs=(vmem,) * 3,
        scratch_shapes=scratch,
        cost_estimate=pl.CostEstimate(
            flops=20 * rows * rank * rank, bytes_accessed=12 * rows * rank, transcendentals=0
        ),
    )(blocks, core_slices)
    second = gram_total(second, depth)
    ortho_basis, factor = pl.pallas_call(
        functools.partial(second_kernel, 1.0 / total_rows),
        out_shape=(tall, square),
        in_specs=[vmem] * 3,
        out_specs=(vmem,) * 2,
        scratch_shapes=scratch + [pltpu.VMEM((rank, rank), F32)],
        cost_estimate=pl.CostEstimate(
            flops=20 * rows * rank * rank, bytes_accessed=12 * rows * rank, transcendentals=0
        ),
    )(second, section, upper_one)
    own_rows = next_core.shape[0]
    factor_mine = lax.dynamic_slice_in_dim(factor, lax.axis_index("wide") * own_rows, own_rows, 0)
    new_core = mul(factor_mine, whole_next, NN)
    return (ortho_basis, new_core)


def solution(mesh):
    return jax.shard_map(
        per_device,
        mesh=mesh,
        in_specs=(P(("wide", "qa", "qb"), None), P("wide", ("qa", "qb"))),
        out_specs=(P(("wide", "qa", "qb"), None), P("wide", ("qa", "qb"))),
        check_vma=False,
    )
```

```python
import functools

import jax
import jax.numpy as jnp
from jax import lax
from jax.experimental import pallas as pl
from jax.experimental.pallas import tpu as pltpu
from jax.sharding import PartitionSpec as P


HALF = 128
SUB = 8
F32 = jnp.float32
NT = (((1,), (1,)), ((), ()))
NN = (((1,), (0,)), ((), ()))
TN = (((0,), (0,)), ((), ()))


def mul(a, b, dims):
    return lax.dot_general(
        a, b, dims, precision=lax.Precision.HIGHEST, preferred_element_type=F32
    )


def row_of(x, j):
    return jnp.broadcast_to(x[j : j + 1, :], x.shape)


def column_of(x, k):
    return jnp.broadcast_to(x[:, k : k + 1], x.shape)


def eliminate(work_ref, upper_ref, inverse_ref, at):
    groups = HALF // SUB
    lane = lax.broadcasted_iota(jnp.int32, (SUB, HALF), 1)
    place = lax.broadcasted_iota(jnp.int32, (SUB, HALF), 0)
    zero = jnp.zeros((SUB, HALF), F32)
    for b in range(groups):
        first = b * SUB
        inside = (lane >= first) & (lane < first + SUB)
        own = work_ref[first : first + SUB, :]
        columns = [column_of(own, first + j) for j in range(SUB)]
        rows = jnp.where(inside, jnp.where(lane - first == place, 1.0, 0.0), own)
        inverses, across, pivots, pivot_rows = [], [], [], []
        for j in range(SUB):
            pivot = row_of(columns[j], j)
            inverse = 1.0 / pivot
            ratio = jnp.where(place > j, columns[j] * inverse, zero)
            ahead = {}
            for i in range(j + 1, SUB):
                ahead[i] = row_of(columns[i], j)
                columns[i] = columns[i] - ratio * ahead[i]
            pivot_row = row_of(rows, j)
            rows = rows - ratio * pivot_row
            inverses.append(inverse)
            across.append(ahead)
            pivots.append(pivot)
            pivot_rows.append(pivot_row)
        for g in range(b + 1, groups):
            other = work_ref[g * SUB : (g + 1) * SUB, :]
            parts = [column_of(other, first + j) for j in range(SUB)]
            other = jnp.where(inside, zero, other)
            for j in range(SUB):
                ratio = parts[j] * inverses[j]
                for i in range(j + 1, SUB):
                    parts[i] = parts[i] - ratio * across[j][i]
                other = other - ratio * pivot_rows[j]
            work_ref[g * SUB : (g + 1) * SUB, :] = other
        pivot_column = pivots[0]
        for j in range(1, SUB):
            pivot_column = jnp.where(place == j, pivots[j], pivot_column)
        root = jnp.sqrt(pivot_column)
        scale = 1.0 / root
        rows = rows * scale
        upper = jnp.where(lane >= first + SUB, rows, zero)
        for j in range(SUB):
            upper = jnp.where((lane == first + j) & (place <= j), columns[j] * scale, upper)
        upper_ref[at + first : at + first + SUB, at : at + HALF] = upper
        inverse_ref[at + first : at + first + SUB, at : at + HALF] = jnp.where(
            lane < first + SUB, rows, zero
        )


def factor_gram(top, side, end, work_ref, upper_ref, inverse_ref):
    work_ref[...] = top
    eliminate(work_ref, upper_ref, inverse_ref, 0)
    inverse_top = inverse_ref[0:HALF, 0:HALF]
    upper_side = mul(inverse_top, side, NN)
    upper_ref[0:HALF, HALF:] = upper_side
    upper_ref[HALF:, 0:HALF] = jnp.zeros((HALF, HALF), F32)
    work_ref[...] = end - mul(upper_side, upper_side, TN)
    carried = mul(upper_side, inverse_top, TN)
    eliminate(work_ref, upper_ref, inverse_ref, HALF)
    inverse_ref[HALF:, 0:HALF] = -mul(inverse_ref[HALF:, HALF:], carried, NN)
    inverse_ref[0:HALF, HALF:] = jnp.zeros((HALF, HALF), F32)


def two_sum(a, b):
    total = a + b
    other = total - a
    return total, (a - (total - other)) + (b - other)


def part(x, anchor):
    return (x + anchor) - anchor


def bf16_dot(a, b):
    return lax.dot_general(a, b, TN, preferred_element_type=F32)


def corners(shape):
    return (
        lax.broadcasted_iota(jnp.int32, shape, 0),
        lax.broadcasted_iota(jnp.int32, shape, 1),
    )


CHUNK = 256
PIECE = HALF + SUB
ANCHOR = 1.5 * 2.0**17
STEP = 2.0**-7


def pack(out_ref, at, square):
    row, column = corners((HALF, HALF))
    top, end = square[0:HALF, 0:HALF], square[HALF:, HALF:]
    diagonal = jnp.sum(jnp.where(row == column, end, 0.0), axis=0, keepdims=True)
    out_ref[0, at : at + HALF, :] = square[0:HALF, HALF:]
    out_ref[0, at + HALF : at + PIECE, :] = jnp.broadcast_to(diagonal, (SUB, HALF))
    out_ref[1, at : at + HALF, :] = jnp.where(row <= column, top, end)
    out_ref[1, at + HALF : at + PIECE, :] = jnp.zeros((SUB, HALF), F32)


def unpack(in_ref, at):
    row, column = corners((HALF, HALF))
    side = in_ref[0, at : at + HALF, :]
    diagonal = in_ref[0, at + HALF : at + HALF + 1, :]
    mixed = in_ref[1, at : at + HALF, :]
    turned = mixed.T
    top = jnp.where(row <= column, mixed, turned)
    end = jnp.where(row > column, mixed, jnp.where(row < column, turned, diagonal))
    return top, side, end


def gram_kernel(core_ref, out_ref, exact_ref, cross_ref, rest_ref, missing_ref):
    largest = jnp.max(jnp.abs(core_ref[...].astype(jnp.bfloat16).astype(F32)), axis=0, keepdims=True)
    anchor = jnp.broadcast_to(largest * ANCHOR, (CHUNK, core_ref.shape[1]))
    exact_ref[...] = jnp.zeros_like(exact_ref)
    cross_ref[...] = jnp.zeros_like(cross_ref)
    rest_ref[...] = jnp.zeros_like(rest_ref)
    missing_ref[...] = jnp.zeros_like(missing_ref)

    @pl.loop(0, core_ref.shape[0] // CHUNK)
    def _(step):
        core = core_ref[pl.ds(pl.multiple_of(step * CHUNK, CHUNK), CHUNK), :]
        halved = core.astype(jnp.bfloat16)
        wide = halved.astype(F32)
        missing = core - wide
        missing_high = missing.astype(jnp.bfloat16)
        missing_wide = missing_high.astype(F32)
        low_wide = missing - missing_wide
        missing_low = low_wide.astype(jnp.bfloat16)
        half_low = (0.5 * low_wide).astype(jnp.bfloat16)
        half_missing = (0.5 * missing_wide).astype(jnp.bfloat16)
        a = part(wide, anchor)
        left = wide - a
        b = part(left, anchor * STEP)
        c = left - b
        low = lambda x: x.astype(jnp.bfloat16)
        a16, b16, c16 = low(a), low(b), low(c)
        half_b, half_c = low(0.5 * b), low(0.5 * c)
        exact_ref[...] += bf16_dot(a16, a16)
        cross_ref[...] += bf16_dot(a16, b16)
        rest_ref[...] += bf16_dot(
            jnp.concatenate([a16, b16, b16, half_c], axis=0),
            jnp.concatenate([c16, half_b, c16, c16], axis=0),
        )
        missing_ref[...] += bf16_dot(
            jnp.concatenate([halved, halved, half_missing, missing_high, half_low], axis=0),
            jnp.concatenate([missing_high, missing_low, missing_high, missing_low, missing_low], axis=0),
        )

    cross, rest, missing = cross_ref[...], rest_ref[...], missing_ref[...]
    high, first = two_sum(exact_ref[...], cross)
    high, second = two_sum(high, cross.T)
    high, third = two_sum(high, rest + rest.T)
    pack(out_ref, 0, high)
    pack(out_ref, PIECE, ((first + second) + third) + (missing + missing.T))


def basis_kernel(scale, gram_ref, core_ref, ortho_ref, factor_ref, work_ref, upper_ref, inverse_ref, lack_ref, other_ref, second_ref):
    top, side, end = (x * scale for x in unpack(gram_ref, 0))
    lack_ref[0:HALF, 0:HALF] = top
    lack_ref[0:HALF, HALF:] = side
    lack_ref[HALF:, 0:HALF] = side.T
    lack_ref[HALF:, HALF:] = end
    factor_gram(top, side, end, work_ref, upper_ref, inverse_ref)

    upper = upper_ref[...]
    anchor = jnp.broadcast_to(jnp.max(jnp.abs(upper), axis=0, keepdims=True) * ANCHOR, upper.shape)
    low = lambda x: x.astype(jnp.bfloat16)
    a = part(upper, anchor)
    left = upper - a
    b = part(left, anchor * STEP)
    left = left - b
    c = part(left, anchor * (STEP * STEP))
    d = left - c
    a16, b16, c16, d16 = low(a), low(b), low(c), low(d)
    half_b, half_c = low(0.5 * b), low(0.5 * c)
    exact = bf16_dot(a16, a16)
    cross = bf16_dot(a16, b16)
    rest = bf16_dot(
        jnp.concatenate([a16, b16, a16, b16, b16, c16, c16], axis=0),
        jnp.concatenate([c16, half_b, d16, c16, d16, half_c, d16], axis=0),
    )
    left, first = two_sum(lack_ref[...], -exact)
    left, second = two_sum(left, -cross)
    left, third = two_sum(left, -cross.T)
    lack_ref[...] = left + (((first + second) + third) - (rest + rest.T))
    top, side, end = (x * scale for x in unpack(gram_ref, PIECE))
    lack_ref[0:HALF, 0:HALF] += top
    lack_ref[0:HALF, HALF:] += side
    lack_ref[HALF:, 0:HALF] += side.T
    lack_ref[HALF:, HALF:] += end

    other_ref[...] = mul(mul(inverse_ref[...], lack_ref[...], NN), inverse_ref[...], NT)
    row, column = corners((HALF, HALF))
    unit = jnp.where(row == column, 1.0, 0.0)
    factor_gram(
        unit + other_ref[0:HALF, 0:HALF],
        other_ref[0:HALF, HALF:],
        unit + other_ref[HALF:, HALF:],
        work_ref,
        second_ref,
        lack_ref,
    )
    factor_ref[...] = mul(second_ref[...], upper_ref[...], NN)
    other_ref[...] = mul(lack_ref[...], inverse_ref[...], NN)

    @pl.loop(0, core_ref.shape[0] // CHUNK)
    def _(step):
        here = pl.ds(pl.multiple_of(step * CHUNK, CHUNK), CHUNK)
        ortho_ref[here, :] = mul(core_ref[here, :], other_ref[...], NT)


def make_calls(rows, rank, scale):
    square = jax.ShapeDtypeStruct((rank, rank), F32)
    tall = jax.ShapeDtypeStruct((rows, rank), F32)
    packed = jax.ShapeDtypeStruct((2, 2 * PIECE, HALF), F32)
    vmem = pl.BlockSpec(memory_space=pltpu.VMEM)
    whole = pltpu.VMEM((rank, rank), F32)
    cost = pl.CostEstimate(
        flops=20 * rows * rank * rank, bytes_accessed=8 * rows * rank, transcendentals=0
    )
    gram = pl.pallas_call(
        gram_kernel,
        out_shape=packed,
        in_specs=[vmem],
        out_specs=vmem,
        scratch_shapes=[whole] * 4,
        cost_estimate=cost,
    )
    basis = pl.pallas_call(
        functools.partial(basis_kernel, scale),
        out_shape=(tall, square),
        in_specs=[vmem] * 2,
        out_specs=(vmem,) * 2,
        scratch_shapes=[pltpu.VMEM((HALF, HALF), F32)] + [whole] * 5,
        cost_estimate=cost,
    )
    return gram, basis


def shifted(value, pairs):
    return lax.ppermute(value, ("wide", "qa", "qb"), pairs)


def add_pairs(x, y):
    high, lost = two_sum(x[:PIECE], y[:PIECE])
    return jnp.concatenate([high, (x[PIECE:] + y[PIECE:]) + lost], axis=0)


def gram_total(pieces):
    depth = 4
    wide, across, cores = (lax.axis_size(n) for n in ("wide", "qa", "qb"))
    long = wide // depth

    def pairs(source):
        out = []
        for i in range(wide * across * cores):
            z, y, x, core = i // (cores * across * depth), i // (cores * across) % depth, i // cores % across, i % cores
            z2, y2, x2, core2 = source(z, y, x, core)
            out.append(((((z2 % long) * depth + y2 % depth) * across + x2 % across) * cores + core2 % cores, i))
        return out

    def around(value, source):
        one, two, three = (shifted(value, pairs(functools.partial(source, d))) for d in (1, 2, -1))
        return add_pairs(add_pairs(value, two), add_pairs(one, three))

    low = lax.axis_index("qb") == 0
    swap = pairs(lambda z, y, x, core: (z, y, x, 1 - core))
    mine = jnp.where(low, pieces[0], pieces[1])
    mine = add_pairs(mine, shifted(jnp.where(low, pieces[1], pieces[0]), swap))
    mine = around(mine, lambda d, z, y, x, core: (z, y, x + d, core) if core == 0 else (z, y + d, x, core))
    mine = around(mine, lambda d, z, y, x, core: (z, y, x + d, core) if core == 1 else (z, y + d, x, core))
    mine = add_pairs(mine, shifted(mine, pairs(lambda z, y, x, core: (z + 4, y, x, core))))
    mine = around(mine, lambda d, z, y, x, core: (z + d, y, x, core))
    other = shifted(mine, swap)
    return jnp.where(low, jnp.stack([mine, other]), jnp.stack([other, mine]))


def per_device(core_slices, next_core):
    rows, rank = core_slices.shape
    total_rows = rows * lax.axis_size("wide") * lax.axis_size("qa") * lax.axis_size("qb")
    gram, basis = make_calls(rows, rank, 1.0 / total_rows)
    whole_next = lax.all_gather(next_core, "wide", axis=0, tiled=True)
    ortho_basis, factor = basis(gram_total(gram(core_slices)), core_slices)
    own_rows = next_core.shape[0]
    factor_mine = lax.dynamic_slice_in_dim(factor, lax.axis_index("wide") * own_rows, own_rows, 0)
    new_core = mul(factor_mine, whole_next, NN)
    return (ortho_basis, new_core)


def solution(mesh):
    return jax.shard_map(
        per_device,
        mesh=mesh,
        in_specs=(P(("wide", "qa", "qb"), None), P("wide", ("qa", "qb"))),
        out_specs=(P(("wide", "qa", "qb"), None), P("wide", ("qa", "qb"))),
        check_vma=False,
    )
```

```python
import functools

import jax
import jax.numpy as jnp
from jax import lax
from jax.experimental import pallas as pl
from jax.experimental.pallas import tpu as pltpu
from jax.sharding import PartitionSpec as P


HALF = 128
SUB = 8
F32 = jnp.float32
NT = (((1,), (1,)), ((), ()))
NN = (((1,), (0,)), ((), ()))
TN = (((0,), (0,)), ((), ()))


def mul(a, b, dims):
    return lax.dot_general(
        a, b, dims, precision=lax.Precision.HIGHEST, preferred_element_type=F32
    )


def row_of(x, j):
    return jnp.broadcast_to(x[j : j + 1, :], x.shape)


def column_of(x, k):
    return jnp.broadcast_to(x[:, k : k + 1], x.shape)


def eliminate(work_ref, upper_ref, inverse_ref, at):
    groups = HALF // SUB
    lane = lax.broadcasted_iota(jnp.int32, (SUB, HALF), 1)
    place = lax.broadcasted_iota(jnp.int32, (SUB, HALF), 0)
    zero = jnp.zeros((SUB, HALF), F32)
    for b in range(groups):
        first = b * SUB
        inside = (lane >= first) & (lane < first + SUB)
        own = work_ref[first : first + SUB, :]
        columns = [column_of(own, first + j) for j in range(SUB)]
        rows = jnp.where(inside, jnp.where(lane - first == place, 1.0, 0.0), own)
        inverses, across, pivots, pivot_rows = [], [], [], []
        for j in range(SUB):
            pivot = row_of(columns[j], j)
            inverse = 1.0 / pivot
            ratio = jnp.where(place > j, columns[j] * inverse, zero)
            ahead = {}
            for i in range(j + 1, SUB):
                ahead[i] = row_of(columns[i], j)
                columns[i] = columns[i] - ratio * ahead[i]
            pivot_row = row_of(rows, j)
            rows = rows - ratio * pivot_row
            inverses.append(inverse)
            across.append(ahead)
            pivots.append(pivot)
            pivot_rows.append(pivot_row)
        for g in range(b + 1, groups):
            other = work_ref[g * SUB : (g + 1) * SUB, :]
            parts = [column_of(other, first + j) for j in range(SUB)]
            other = jnp.where(inside, zero, other)
            for j in range(SUB):
                ratio = parts[j] * inverses[j]
                for i in range(j + 1, SUB):
                    parts[i] = parts[i] - ratio * across[j][i]
                other = other - ratio * pivot_rows[j]
            work_ref[g * SUB : (g + 1) * SUB, :] = other
        pivot_column = pivots[0]
        for j in range(1, SUB):
            pivot_column = jnp.where(place == j, pivots[j], pivot_column)
        root = jnp.sqrt(pivot_column)
        scale = 1.0 / root
        rows = rows * scale
        upper = jnp.where(lane >= first + SUB, rows, zero)
        for j in range(SUB):
            upper = jnp.where((lane == first + j) & (place <= j), columns[j] * scale, upper)
        upper_ref[at + first : at + first + SUB, at : at + HALF] = upper
        inverse_ref[at + first : at + first + SUB, at : at + HALF] = jnp.where(
            lane < first + SUB, rows, zero
        )


def factor_gram(top, side, end, work_ref, upper_ref, inverse_ref):
    work_ref[...] = top
    eliminate(work_ref, upper_ref, inverse_ref, 0)
    inverse_top = inverse_ref[0:HALF, 0:HALF]
    upper_side = mul(inverse_top, side, NN)
    upper_ref[0:HALF, HALF:] = upper_side
    upper_ref[HALF:, 0:HALF] = jnp.zeros((HALF, HALF), F32)
    work_ref[...] = end - mul(upper_side, upper_side, TN)
    carried = mul(upper_side, inverse_top, TN)
    eliminate(work_ref, upper_ref, inverse_ref, HALF)
    inverse_ref[HALF:, 0:HALF] = -mul(inverse_ref[HALF:, HALF:], carried, NN)
    inverse_ref[0:HALF, HALF:] = jnp.zeros((HALF, HALF), F32)


def two_sum(a, b):
    total = a + b
    other = total - a
    return total, (a - (total - other)) + (b - other)


def part(x, anchor):
    return (x + anchor) - anchor


def bf16_dot(a, b):
    return lax.dot_general(a, b, TN, preferred_element_type=F32)


def corners(shape):
    return (
        lax.broadcasted_iota(jnp.int32, shape, 0),
        lax.broadcasted_iota(jnp.int32, shape, 1),
    )


CHUNK = 256
PIECE = HALF + SUB
ANCHOR = 1.5 * 2.0**17
STEP = 2.0**-7


def pack(out_ref, at, square):
    row, column = corners((HALF, HALF))
    top, end = square[0:HALF, 0:HALF], square[HALF:, HALF:]
    diagonal = jnp.sum(jnp.where(row == column, end, 0.0), axis=0, keepdims=True)
    out_ref[0, at : at + HALF, :] = square[0:HALF, HALF:]
    out_ref[0, at + HALF : at + PIECE, :] = jnp.broadcast_to(diagonal, (SUB, HALF))
    out_ref[1, at : at + HALF, :] = jnp.where(row <= column, top, end)
    out_ref[1, at + HALF : at + PIECE, :] = jnp.zeros((SUB, HALF), F32)


def unpack(in_ref, at):
    row, column = corners((HALF, HALF))
    side = in_ref[0, at : at + HALF, :]
    diagonal = in_ref[0, at + HALF : at + HALF + 1, :]
    mixed = in_ref[1, at : at + HALF, :]
    turned = mixed.T
    top = jnp.where(row <= column, mixed, turned)
    end = jnp.where(row > column, mixed, jnp.where(row < column, turned, diagonal))
    return top, side, end


def gram_kernel(core_ref, out_ref, exact_ref, cross_ref, rest_ref, missing_ref):
    largest = jnp.max(jnp.abs(core_ref[...].astype(jnp.bfloat16).astype(F32)), axis=0, keepdims=True)
    anchor = jnp.broadcast_to(largest * ANCHOR, (CHUNK, core_ref.shape[1]))
    exact_ref[...] = jnp.zeros_like(exact_ref)
    cross_ref[...] = jnp.zeros_like(cross_ref)
    rest_ref[...] = jnp.zeros_like(rest_ref)
    missing_ref[...] = jnp.zeros_like(missing_ref)

    @pl.loop(0, core_ref.shape[0] // CHUNK)
    def _(step):
        core = core_ref[pl.ds(pl.multiple_of(step * CHUNK, CHUNK), CHUNK), :]
        halved = core.astype(jnp.bfloat16)
        wide = halved.astype(F32)
        missing = core - wide
        missing_high = missing.astype(jnp.bfloat16)
        missing_wide = missing_high.astype(F32)
        low_wide = missing - missing_wide
        missing_low = low_wide.astype(jnp.bfloat16)
        half_low = (0.5 * low_wide).astype(jnp.bfloat16)
        half_missing = (0.5 * missing_wide).astype(jnp.bfloat16)
        a = part(wide, anchor)
        left = wide - a
        b = part(left, anchor * STEP)
        c = left - b
        low = lambda x: x.astype(jnp.bfloat16)
        a16, b16, c16 = low(a), low(b), low(c)
        half_b, half_c = low(0.5 * b), low(0.5 * c)
        exact_ref[...] += bf16_dot(a16, a16)
        cross_ref[...] += bf16_dot(a16, b16)
        rest_ref[...] += bf16_dot(
            jnp.concatenate([a16, b16, b16, half_c], axis=0),
            jnp.concatenate([c16, half_b, c16, c16], axis=0),
        )
        missing_ref[...] += bf16_dot(
            jnp.concatenate([halved, halved, half_missing, missing_high, half_low], axis=0),
            jnp.concatenate([missing_high, missing_low, missing_high, missing_low, missing_low], axis=0),
        )

    cross, rest, missing = cross_ref[...], rest_ref[...], missing_ref[...]
    high, first = two_sum(exact_ref[...], cross)
    high, second = two_sum(high, cross.T)
    high, third = two_sum(high, rest + rest.T)
    pack(out_ref, 0, high)
    pack(out_ref, PIECE, ((first + second) + third) + (missing + missing.T))


def basis_kernel(scale, place_ref, gram_ref, core_ref, order_ref, ortho_ref, factor_ref, work_ref, upper_ref, inverse_ref, lack_ref, other_ref, second_ref):
    top, side, end = (x * scale for x in unpack(gram_ref, 0))
    lack_ref[0:HALF, 0:HALF] = top
    lack_ref[0:HALF, HALF:] = side
    lack_ref[HALF:, 0:HALF] = side.T
    lack_ref[HALF:, HALF:] = end
    factor_gram(top, side, end, work_ref, upper_ref, inverse_ref)

    upper = upper_ref[...]
    anchor = jnp.broadcast_to(jnp.max(jnp.abs(upper), axis=0, keepdims=True) * ANCHOR, upper.shape)
    low = lambda x: x.astype(jnp.bfloat16)
    a = part(upper, anchor)
    left = upper - a
    b = part(left, anchor * STEP)
    left = left - b
    c = part(left, anchor * (STEP * STEP))
    d = left - c
    a16, b16, c16, d16 = low(a), low(b), low(c), low(d)
    half_b, half_c = low(0.5 * b), low(0.5 * c)
    exact = bf16_dot(a16, a16)
    cross = bf16_dot(a16, b16)
    rest = bf16_dot(
        jnp.concatenate([a16, b16, a16, b16, b16, c16, c16], axis=0),
        jnp.concatenate([c16, half_b, d16, c16, d16, half_c, d16], axis=0),
    )
    left, first = two_sum(lack_ref[...], -exact)
    left, second = two_sum(left, -cross)
    left, third = two_sum(left, -cross.T)
    lack_ref[...] = left + (((first + second) + third) - (rest + rest.T))
    top, side, end = (x * scale for x in unpack(gram_ref, PIECE))
    lack_ref[0:HALF, 0:HALF] += top
    lack_ref[0:HALF, HALF:] += side
    lack_ref[HALF:, 0:HALF] += side.T
    lack_ref[HALF:, HALF:] += end

    other_ref[...] = mul(mul(inverse_ref[...], lack_ref[...], NN), inverse_ref[...], NT)
    row, column = corners((HALF, HALF))
    unit = jnp.where(row == column, 1.0, 0.0)
    factor_gram(
        unit + other_ref[0:HALF, 0:HALF],
        other_ref[0:HALF, HALF:],
        unit + other_ref[HALF:, HALF:],
        work_ref,
        second_ref,
        lack_ref,
    )
    mine = second_ref[pl.ds(pl.multiple_of(place_ref[0] * SUB, SUB), SUB), :]
    factor_ref[...] = mul(mul(mine, upper_ref[...], NN), order_ref[...], NN)
    other_ref[...] = mul(lack_ref[...], inverse_ref[...], NN)

    @pl.loop(0, core_ref.shape[0] // CHUNK)
    def _(step):
        here = pl.ds(pl.multiple_of(step * CHUNK, CHUNK), CHUNK)
        ortho_ref[here, :] = mul(core_ref[here, :], other_ref[...], NT)


def next_kernel(factor_ref, own_ref, right_ref, left_ref, far_low_ref, far_high_ref, out_ref):
    low = lambda x: x.astype(jnp.bfloat16)
    factor = factor_ref[...]
    first = low(factor)
    left = factor - first.astype(F32)
    second = low(left)
    third = low(left - second.astype(F32))
    stacked = jnp.concatenate([first.astype(F32), second.astype(F32), third.astype(F32)], axis=0)
    stacked = low(stacked)
    wide = 256

    @pl.loop(0, out_ref.shape[1] // wide)
    def _(step):
        here = pl.ds(pl.multiple_of(step * wide, wide), wide)
        pieces = (own_ref, right_ref, left_ref, far_low_ref, far_high_ref)
        values = jnp.concatenate([piece[:, here] for piece in pieces], axis=0)
        high = low(values)
        rest = low(values - high.astype(F32))
        dot = lambda b: lax.dot_general(stacked, b, NN, preferred_element_type=F32)
        whole = dot(high) + dot(rest)
        out_ref[:, here] = whole[0:SUB] + (whole[SUB : 2 * SUB] + whole[2 * SUB :])


def make_calls(rows, rank, scale, own_rows=SUB):
    tall = jax.ShapeDtypeStruct((rows, rank), F32)
    packed = jax.ShapeDtypeStruct((2, 2 * PIECE, HALF), F32)
    vmem = pl.BlockSpec(memory_space=pltpu.VMEM)
    whole = pltpu.VMEM((rank, rank), F32)
    cost = pl.CostEstimate(
        flops=20 * rows * rank * rank, bytes_accessed=8 * rows * rank, transcendentals=0
    )
    gram = pl.pallas_call(
        gram_kernel,
        out_shape=packed,
        in_specs=[vmem],
        out_specs=vmem,
        scratch_shapes=[whole] * 4,
        cost_estimate=cost,
    )
    basis = pl.pallas_call(
        functools.partial(basis_kernel, scale),
        out_shape=(tall, jax.ShapeDtypeStruct((own_rows, rank), F32)),
        in_specs=[pl.BlockSpec(memory_space=pltpu.SMEM)] + [vmem] * 3,
        out_specs=(vmem,) * 2,
        scratch_shapes=[pltpu.VMEM((HALF, HALF), F32)] + [whole] * 5,
        cost_estimate=cost,
    )
    return gram, basis


def shifted(value, pairs):
    return lax.ppermute(value, ("wide", "qa", "qb"), pairs)


def add_pairs(x, y):
    high, lost = two_sum(x[:PIECE], y[:PIECE])
    return jnp.concatenate([high, (x[PIECE:] + y[PIECE:]) + lost], axis=0)


def tie(*values):
    return lax.optimization_barrier(values)


def sum_and_spread(pieces, next_core):
    depth = 4
    wide, across, cores = (lax.axis_size(n) for n in ("wide", "qa", "qb"))
    long = wide // depth
    z_bits = lax.axis_index("wide") // depth

    def pairs(source):
        out = []
        for i in range(wide * across * cores):
            z, y, x, core = i // (cores * across * depth), i // (cores * across) % depth, i // cores % across, i % cores
            z2, y2, x2, core2 = source(z, y, x, core)
            out.append(((((z2 % long) * depth + y2 % depth) * across + x2 % across) * cores + core2 % cores, i))
        return out

    def around(value, source):
        one, two, three = (shifted(value, pairs(functools.partial(source, d))) for d in (1, 2, -1))
        return add_pairs(add_pairs(value, two), add_pairs(one, three))

    def partner(value, bit):
        return shifted(value, pairs(lambda z, y, x, core: (z ^ bit, y, x, core)))

    def merge(own, other, bit):
        first = (z_bits & bit) == 0
        return jnp.concatenate([jnp.where(first, own, other), jnp.where(first, other, own)], axis=0)

    def beside(value, d):
        return shifted(value, pairs(lambda z, y, x, core: (z, y + d, x, core)))

    low = lax.axis_index("qb") == 0
    swap = pairs(lambda z, y, x, core: (z, y, x, 1 - core))
    other = partner(next_core, 4)
    mine = jnp.where(low, pieces[0], pieces[1])
    mine = add_pairs(mine, shifted(jnp.where(low, pieces[1], pieces[0]), swap))
    mine, other = tie(mine, other)
    rows = merge(next_core, other, 4)
    other = partner(rows, 2)
    mine = around(mine, lambda d, z, y, x, core: (z, y, x + d, core) if core == 0 else (z, y + d, x, core))
    mine, other = tie(mine, other)
    rows = merge(rows, other, 2)
    other = partner(rows, 1)
    mine = around(mine, lambda d, z, y, x, core: (z, y, x + d, core) if core == 1 else (z, y + d, x, core))
    mine, other = tie(mine, other)
    rows = merge(rows, other, 1)
    right, left = beside(rows, -1), beside(rows, 1)
    mine = add_pairs(mine, shifted(mine, pairs(lambda z, y, x, core: (z + 4, y, x, core))))
    mine = around(mine, lambda d, z, y, x, core: (z + d, y, x, core))
    other = shifted(mine, swap)
    total = jnp.where(low, jnp.stack([mine, other]), jnp.stack([other, mine]))
    total, right, left = tie(total, right, left)
    half = rows.shape[0] // 2
    far_low, far_high = beside(right[:half], -1), beside(left[half:], 1)
    return total, (rows, right, left, far_low, far_high)


def row_order(rank, own_rows):
    depth, long = 4, lax.axis_size("wide") // 4
    at = jnp.arange(rank)
    quarter, z, row = at // (long * own_rows), at // own_rows % long, at % own_rows
    z = (z & 1) * 4 + (z & 2) + (z >> 2)
    shift = jnp.where(quarter == 1, -1, jnp.where(quarter == 2, 1, jnp.where(quarter == 3, 2, 0)))
    y = (lax.axis_index("wide") % depth + shift + depth) % depth
    source = (z * depth + y) * own_rows + row
    return (at[:, None] == source[None, :]).astype(F32)


def per_device(core_slices, next_core):
    rows, rank = core_slices.shape
    own_rows = next_core.shape[0]
    total_rows = rows * lax.axis_size("wide") * lax.axis_size("qa") * lax.axis_size("qb")
    gram, basis = make_calls(rows, rank, 1.0 / total_rows, own_rows)
    total, pieces = sum_and_spread(gram(core_slices), next_core)
    place = jnp.reshape(lax.axis_index("wide").astype(jnp.int32), (1,))
    ortho_basis, factor = basis(place, total, core_slices, row_order(rank, own_rows))
    vmem = pl.BlockSpec(memory_space=pltpu.VMEM)
    new_core = pl.pallas_call(
        next_kernel,
        out_shape=jax.ShapeDtypeStruct(next_core.shape, F32),
        in_specs=[vmem] * 6,
        out_specs=vmem,
    )(factor, *pieces)
    return (ortho_basis, new_core)


def solution(mesh):
    return jax.shard_map(
        per_device,
        mesh=mesh,
        in_specs=(P(("wide", "qa", "qb"), None), P("wide", ("qa", "qb"))),
        out_specs=(P(("wide", "qa", "qb"), None), P("wide", ("qa", "qb"))),
        check_vma=False,
    )
```

```python
import functools

import jax
import jax.numpy as jnp
from jax import lax
from jax.experimental import pallas as pl
from jax.experimental.pallas import tpu as pltpu
from jax.sharding import PartitionSpec as P


HALF = 128
SUB = 8
F32 = jnp.float32
NT = (((1,), (1,)), ((), ()))
NN = (((1,), (0,)), ((), ()))
TN = (((0,), (0,)), ((), ()))


def mul(a, b, dims):
    return lax.dot_general(
        a, b, dims, precision=lax.Precision.HIGHEST, preferred_element_type=F32
    )


def row_of(x, j):
    return jnp.broadcast_to(x[j : j + 1, :], x.shape)


def column_of(x, k):
    return jnp.broadcast_to(x[:, k : k + 1], x.shape)


def eliminate(work_ref, upper_ref, inverse_ref, at):
    groups = HALF // SUB
    lane = lax.broadcasted_iota(jnp.int32, (SUB, HALF), 1)
    place = lax.broadcasted_iota(jnp.int32, (SUB, HALF), 0)
    zero = jnp.zeros((SUB, HALF), F32)
    for b in range(groups):
        first = b * SUB
        inside = (lane >= first) & (lane < first + SUB)
        own = work_ref[first : first + SUB, :]
        columns = [column_of(own, first + j) for j in range(SUB)]
        rows = jnp.where(inside, jnp.where(lane - first == place, 1.0, 0.0), own)
        inverses, across, pivots, pivot_rows = [], [], [], []
        for j in range(SUB):
            pivot = row_of(columns[j], j)
            inverse = 1.0 / pivot
            ratio = jnp.where(place > j, columns[j] * inverse, zero)
            ahead = {}
            for i in range(j + 1, SUB):
                ahead[i] = row_of(columns[i], j)
                columns[i] = columns[i] - ratio * ahead[i]
            pivot_row = row_of(rows, j)
            rows = rows - ratio * pivot_row
            inverses.append(inverse)
            across.append(ahead)
            pivots.append(pivot)
            pivot_rows.append(pivot_row)
        for g in range(b + 1, groups):
            other = work_ref[g * SUB : (g + 1) * SUB, :]
            parts = [column_of(other, first + j) for j in range(SUB)]
            other = jnp.where(inside, zero, other)
            for j in range(SUB):
                ratio = parts[j] * inverses[j]
                for i in range(j + 1, SUB):
                    parts[i] = parts[i] - ratio * across[j][i]
                other = other - ratio * pivot_rows[j]
            work_ref[g * SUB : (g + 1) * SUB, :] = other
        pivot_column = pivots[0]
        for j in range(1, SUB):
            pivot_column = jnp.where(place == j, pivots[j], pivot_column)
        root = jnp.sqrt(pivot_column)
        scale = 1.0 / root
        rows = rows * scale
        upper = jnp.where(lane >= first + SUB, rows, zero)
        for j in range(SUB):
            upper = jnp.where((lane == first + j) & (place <= j), columns[j] * scale, upper)
        upper_ref[at + first : at + first + SUB, at : at + HALF] = upper
        inverse_ref[at + first : at + first + SUB, at : at + HALF] = jnp.where(
            lane < first + SUB, rows, zero
        )


def factor_gram(top, side, end, work_ref, upper_ref, inverse_ref):
    work_ref[...] = top
    eliminate(work_ref, upper_ref, inverse_ref, 0)
    inverse_top = inverse_ref[0:HALF, 0:HALF]
    upper_side = mul(inverse_top, side, NN)
    upper_ref[0:HALF, HALF:] = upper_side
    upper_ref[HALF:, 0:HALF] = jnp.zeros((HALF, HALF), F32)
    work_ref[...] = end - mul(upper_side, upper_side, TN)
    carried = mul(upper_side, inverse_top, TN)
    eliminate(work_ref, upper_ref, inverse_ref, HALF)
    inverse_ref[HALF:, 0:HALF] = -mul(inverse_ref[HALF:, HALF:], carried, NN)
    inverse_ref[0:HALF, HALF:] = jnp.zeros((HALF, HALF), F32)


def two_sum(a, b):
    total = a + b
    other = total - a
    return total, (a - (total - other)) + (b - other)


def part(x, anchor):
    return (x + anchor) - anchor


def bf16_dot(a, b):
    return lax.dot_general(a, b, TN, preferred_element_type=F32)


def corners(shape):
    return (
        lax.broadcasted_iota(jnp.int32, shape, 0),
        lax.broadcasted_iota(jnp.int32, shape, 1),
    )


CHUNK = 256
PIECE = HALF + SUB
ANCHOR = 1.5 * 2.0**17
STEP = 2.0**-7


def pack(mine_ref, theirs_ref, at, square, low):
    row, column = corners((HALF, HALF))
    top, end = square[0:HALF, 0:HALF], square[HALF:, HALF:]
    diagonal = jnp.sum(jnp.where(row == column, end, 0.0), axis=0, keepdims=True)
    side = square[0:HALF, HALF:]
    mixed = jnp.where(row <= column, top, end)
    diagonal = jnp.broadcast_to(diagonal, (SUB, HALF))
    mine_ref[at : at + HALF, :] = jnp.where(low, side, mixed)
    theirs_ref[at : at + HALF, :] = jnp.where(low, mixed, side)
    mine_ref[at + HALF : at + PIECE, :] = diagonal
    theirs_ref[at + HALF : at + PIECE, :] = diagonal


def unpack(mine_ref, theirs_ref, at, low):
    row, column = corners((HALF, HALF))
    mine, theirs = mine_ref[at : at + HALF, :], theirs_ref[at : at + HALF, :]
    side = jnp.where(low, mine, theirs)
    mixed = jnp.where(low, theirs, mine)
    edge = slice(at + HALF, at + HALF + 1)
    diagonal = jnp.where(low, mine_ref[edge, :], theirs_ref[edge, :])
    turned = mixed.T
    top = jnp.where(row <= column, mixed, turned)
    end = jnp.where(row > column, mixed, jnp.where(row < column, turned, diagonal))
    return top, side, end


def gram_kernel(place_ref, core_ref, mine_ref, theirs_ref, exact_ref, cross_ref, rest_ref, missing_ref):
    largest = jnp.max(jnp.abs(core_ref[...].astype(jnp.bfloat16).astype(F32)), axis=0, keepdims=True)
    anchor = jnp.broadcast_to(largest * ANCHOR, (CHUNK, core_ref.shape[1]))
    exact_ref[...] = jnp.zeros_like(exact_ref)
    cross_ref[...] = jnp.zeros_like(cross_ref)
    rest_ref[...] = jnp.zeros_like(rest_ref)
    missing_ref[...] = jnp.zeros_like(missing_ref)

    @pl.loop(0, core_ref.shape[0] // CHUNK)
    def _(step):
        core = core_ref[pl.ds(pl.multiple_of(step * CHUNK, CHUNK), CHUNK), :]
        halved = core.astype(jnp.bfloat16)
        wide = halved.astype(F32)
        missing = core - wide
        missing_high = missing.astype(jnp.bfloat16)
        missing_wide = missing_high.astype(F32)
        low_wide = missing - missing_wide
        missing_low = low_wide.astype(jnp.bfloat16)
        half_low = (0.5 * low_wide).astype(jnp.bfloat16)
        half_missing = (0.5 * missing_wide).astype(jnp.bfloat16)
        a = part(wide, anchor)
        left = wide - a
        b = part(left, anchor * STEP)
        c = left - b
        low = lambda x: x.astype(jnp.bfloat16)
        a16, b16, c16 = low(a), low(b), low(c)
        half_b, half_c = low(0.5 * b), low(0.5 * c)
        exact_ref[...] += bf16_dot(a16, a16)
        cross_ref[...] += bf16_dot(a16, b16)
        rest_ref[...] += bf16_dot(
            jnp.concatenate([a16, b16, b16, half_c], axis=0),
            jnp.concatenate([c16, half_b, c16, c16], axis=0),
        )
        missing_ref[...] += bf16_dot(
            jnp.concatenate([halved, halved, half_missing, missing_high, half_low], axis=0),
            jnp.concatenate([missing_high, missing_low, missing_high, missing_low, missing_low], axis=0),
        )

    cross, rest, missing = cross_ref[...], rest_ref[...], missing_ref[...]
    high, first = two_sum(exact_ref[...], cross)
    high, second = two_sum(high, cross.T)
    high, third = two_sum(high, rest + rest.T)
    low_core = place_ref[1] == 0
    pack(mine_ref, theirs_ref, 0, high, low_core)
    pack(mine_ref, theirs_ref, PIECE, ((first + second) + third) + (missing + missing.T), low_core)


def piece_order(place, rank, own_rows):
    depth = 4
    long = rank // (depth * own_rows)
    source, at = corners((rank, rank))
    quarter, z, row = at // (long * own_rows), at // own_rows % long, at % own_rows
    z = (z & 1) * 4 + (z & 2) + (z >> 2)
    shift = jnp.where(quarter == 1, depth - 1, jnp.where(quarter == 2, 1, jnp.where(quarter == 3, 2, 0)))
    y = (place + shift) & (depth - 1)
    return jnp.where(source == (z * depth + y) * own_rows + row, 1.0, 0.0)


def basis_kernel(scale, place_ref, mine_ref, theirs_ref, core_ref, ortho_ref, factor_ref, work_ref, upper_ref, inverse_ref, lack_ref, other_ref, second_ref):
    low_core = place_ref[1] == 0
    top, side, end = (x * scale for x in unpack(mine_ref, theirs_ref, 0, low_core))
    lack_ref[0:HALF, 0:HALF] = top
    lack_ref[0:HALF, HALF:] = side
    lack_ref[HALF:, 0:HALF] = side.T
    lack_ref[HALF:, HALF:] = end
    factor_gram(top, side, end, work_ref, upper_ref, inverse_ref)

    upper = upper_ref[...]
    anchor = jnp.broadcast_to(jnp.max(jnp.abs(upper), axis=0, keepdims=True) * ANCHOR, upper.shape)
    low = lambda x: x.astype(jnp.bfloat16)
    a = part(upper, anchor)
    left = upper - a
    b = part(left, anchor * STEP)
    left = left - b
    c = part(left, anchor * (STEP * STEP))
    d = left - c
    a16, b16, c16, d16 = low(a), low(b), low(c), low(d)
    half_b, half_c = low(0.5 * b), low(0.5 * c)
    exact = bf16_dot(a16, a16)
    cross = bf16_dot(a16, b16)
    rest = bf16_dot(
        jnp.concatenate([a16, b16, a16, b16, b16, c16, c16], axis=0),
        jnp.concatenate([c16, half_b, d16, c16, d16, half_c, d16], axis=0),
    )
    left, first = two_sum(lack_ref[...], -exact)
    left, second = two_sum(left, -cross)
    left, third = two_sum(left, -cross.T)
    lack_ref[...] = left + (((first + second) + third) - (rest + rest.T))
    top, side, end = (x * scale for x in unpack(mine_ref, theirs_ref, PIECE, low_core))
    lack_ref[0:HALF, 0:HALF] += top
    lack_ref[0:HALF, HALF:] += side
    lack_ref[HALF:, 0:HALF] += side.T
    lack_ref[HALF:, HALF:] += end

    other_ref[...] = mul(mul(inverse_ref[...], lack_ref[...], NN), inverse_ref[...], NT)
    row, column = corners((HALF, HALF))
    unit = jnp.where(row == column, 1.0, 0.0)
    factor_gram(
        unit + other_ref[0:HALF, 0:HALF],
        other_ref[0:HALF, HALF:],
        unit + other_ref[HALF:, HALF:],
        work_ref,
        second_ref,
        lack_ref,
    )
    mine = second_ref[pl.ds(pl.multiple_of(place_ref[0] * SUB, SUB), SUB), :]
    order = piece_order(place_ref[0], core_ref.shape[1], factor_ref.shape[0])
    factor_ref[...] = mul(mul(mine, upper_ref[...], NN), order, NN)
    other_ref[...] = mul(lack_ref[...], inverse_ref[...], NN)

    @pl.loop(0, core_ref.shape[0] // CHUNK)
    def _(step):
        here = pl.ds(pl.multiple_of(step * CHUNK, CHUNK), CHUNK)
        ortho_ref[here, :] = mul(core_ref[here, :], other_ref[...], NT)


def next_kernel(factor_ref, own_ref, right_ref, left_ref, far_low_ref, far_high_ref, out_ref):
    low = lambda x: x.astype(jnp.bfloat16)
    factor = factor_ref[...]
    first = low(factor)
    left = factor - first.astype(F32)
    second = low(left)
    third = low(left - second.astype(F32))
    stacked = jnp.concatenate([first.astype(F32), second.astype(F32), third.astype(F32)], axis=0)
    stacked = low(stacked)
    wide = 256

    for step in range(out_ref.shape[1] // wide):
        here = slice(step * wide, (step + 1) * wide)
        pieces = (own_ref, right_ref, left_ref, far_low_ref, far_high_ref)
        values = jnp.concatenate([piece[:, here] for piece in pieces], axis=0)
        high = low(values)
        rest = low(values - high.astype(F32))
        dot = lambda b: lax.dot_general(stacked, b, NN, preferred_element_type=F32)
        whole = dot(high) + dot(rest)
        out_ref[:, here] = whole[0:SUB] + (whole[SUB : 2 * SUB] + whole[2 * SUB :])


def make_calls(rows, rank, scale, own_rows=SUB):
    tall = jax.ShapeDtypeStruct((rows, rank), F32)
    packed = jax.ShapeDtypeStruct((2 * PIECE, HALF), F32)
    smem = pl.BlockSpec(memory_space=pltpu.SMEM)
    vmem = pl.BlockSpec(memory_space=pltpu.VMEM)
    whole = pltpu.VMEM((rank, rank), F32)
    cost = pl.CostEstimate(
        flops=20 * rows * rank * rank, bytes_accessed=8 * rows * rank, transcendentals=0
    )
    gram = pl.pallas_call(
        gram_kernel,
        out_shape=(packed, packed),
        in_specs=[smem, vmem],
        out_specs=(vmem, vmem),
        scratch_shapes=[whole] * 4,
        cost_estimate=cost,
    )
    basis = pl.pallas_call(
        functools.partial(basis_kernel, scale),
        out_shape=(tall, jax.ShapeDtypeStruct((own_rows, rank), F32)),
        in_specs=[smem] + [vmem] * 3,
        out_specs=(vmem,) * 2,
        scratch_shapes=[pltpu.VMEM((HALF, HALF), F32)] + [whole] * 5,
        cost_estimate=cost,
    )
    return gram, basis


def shifted(value, pairs):
    return lax.ppermute(value, ("wide", "qa", "qb"), pairs)


def add_pairs(x, y):
    high, lost = two_sum(x[:PIECE], y[:PIECE])
    return jnp.concatenate([high, (x[PIECE:] + y[PIECE:]) + lost], axis=0)


def tie(*values):
    return lax.optimization_barrier(values)


def sum_and_spread(place, gram, core_slices, next_core):
    depth = 4
    wide, across, cores = (lax.axis_size(n) for n in ("wide", "qa", "qb"))
    long = wide // depth
    z_bits = lax.axis_index("wide") // depth

    def pairs(source):
        out = []
        for i in range(wide * across * cores):
            z, y, x, core = i // (cores * across * depth), i // (cores * across) % depth, i // cores % across, i % cores
            z2, y2, x2, core2 = source(z, y, x, core)
            out.append(((((z2 % long) * depth + y2 % depth) * across + x2 % across) * cores + core2 % cores, i))
        return out

    def around(value, source):
        one, two, three = (shifted(value, pairs(functools.partial(source, d))) for d in (1, 2, -1))
        return add_pairs(add_pairs(value, two), add_pairs(one, three))

    def partner(value, bit):
        return shifted(value, pairs(lambda z, y, x, core: (z ^ bit, y, x, core)))

    def merge(own, other, bit):
        first = (z_bits & bit) == 0
        return jnp.concatenate([jnp.where(first, own, other), jnp.where(first, other, own)], axis=0)

    def beside(value, d):
        return shifted(value, pairs(lambda z, y, x, core: (z, y + d, x, core)))

    swap = pairs(lambda z, y, x, core: (z, y, x, 1 - core))
    other = partner(next_core, 4)
    mine, theirs = gram(place, core_slices)
    mine = add_pairs(mine, shifted(theirs, swap))
    mine, other = tie(mine, other)
    rows = merge(next_core, other, 4)
    other = partner(rows, 2)
    mine = around(mine, lambda d, z, y, x, core: (z, y, x + d, core) if core == 0 else (z, y + d, x, core))
    mine, other = tie(mine, other)
    rows = merge(rows, other, 2)
    other = partner(rows, 1)
    mine = around(mine, lambda d, z, y, x, core: (z, y, x + d, core) if core == 1 else (z, y + d, x, core))
    mine, other = tie(mine, other)
    rows = merge(rows, other, 1)
    right = beside(rows, -1)
    left = beside(rows, 1)
    other = shifted(mine, pairs(lambda z, y, x, core: (z + 4, y, x, core)))
    mine = add_pairs(mine, other)
    mine = around(mine, lambda d, z, y, x, core: (z + d, y, x, core))
    theirs = shifted(mine, swap)
    mine, theirs, right, left = tie(mine, theirs, right, left)
    half = rows.shape[0] // 2
    far_low, far_high = beside(right[:half], -1), beside(left[half:], 1)
    return (mine, theirs), (rows, right, left, far_low, far_high)


def per_device(core_slices, next_core):
    rows, rank = core_slices.shape
    own_rows = next_core.shape[0]
    total_rows = rows * lax.axis_size("wide") * lax.axis_size("qa") * lax.axis_size("qb")
    gram, basis = make_calls(rows, rank, 1.0 / total_rows, own_rows)
    vmem = pl.BlockSpec(memory_space=pltpu.VMEM)
    place = jnp.stack([lax.axis_index("wide"), lax.axis_index("qb")]).astype(jnp.int32)
    total, pieces = sum_and_spread(place, gram, core_slices, next_core)
    ortho_basis, factor = basis(place, *total, core_slices)
    new_core = pl.pallas_call(
        next_kernel,
        out_shape=jax.ShapeDtypeStruct(next_core.shape, F32),
        in_specs=[vmem] * 6,
        out_specs=vmem,
    )(factor, *pieces)
    return (ortho_basis, new_core)


def solution(mesh):
    return jax.shard_map(
        per_device,
        mesh=mesh,
        in_specs=(P(("wide", "qa", "qb"), None), P("wide", ("qa", "qb"))),
        out_specs=(P(("wide", "qa", "qb"), None), P("wide", ("qa", "qb"))),
        check_vma=False,
    )
```

```python
import functools

import jax
import jax.numpy as jnp
from jax import lax
from jax.experimental import pallas as pl
from jax.experimental.pallas import tpu as pltpu
from jax.sharding import PartitionSpec as P


HALF = 128
SUB = 8
F32 = jnp.float32
NT = (((1,), (1,)), ((), ()))
NN = (((1,), (0,)), ((), ()))
TN = (((0,), (0,)), ((), ()))


def mul(a, b, dims):
    return lax.dot_general(
        a, b, dims, precision=lax.Precision.HIGHEST, preferred_element_type=F32
    )


def row_of(x, j):
    return jnp.broadcast_to(x[j : j + 1, :], x.shape)


def column_of(x, k):
    return jnp.broadcast_to(x[:, k : k + 1], x.shape)


def eliminate(work_ref, upper_ref, inverse_ref, at):
    groups = HALF // SUB
    lane = lax.broadcasted_iota(jnp.int32, (SUB, HALF), 1)
    place = lax.broadcasted_iota(jnp.int32, (SUB, HALF), 0)
    zero = jnp.zeros((SUB, HALF), F32)
    for b in range(groups):
        first = b * SUB
        inside = (lane >= first) & (lane < first + SUB)
        own = work_ref[first : first + SUB, :]
        columns = [column_of(own, first + j) for j in range(SUB)]
        rows = jnp.where(inside, jnp.where(lane - first == place, 1.0, 0.0), own)
        inverses, across, pivots, pivot_rows = [], [], [], []
        for j in range(SUB):
            pivot = row_of(columns[j], j)
            inverse = 1.0 / pivot
            ratio = jnp.where(place > j, columns[j] * inverse, zero)
            ahead = {}
            for i in range(j + 1, SUB):
                ahead[i] = row_of(columns[i], j)
                columns[i] = columns[i] - ratio * ahead[i]
            pivot_row = row_of(rows, j)
            rows = rows - ratio * pivot_row
            inverses.append(inverse)
            across.append(ahead)
            pivots.append(pivot)
            pivot_rows.append(pivot_row)
        for g in range(b + 1, groups):
            other = work_ref[g * SUB : (g + 1) * SUB, :]
            parts = [column_of(other, first + j) for j in range(SUB)]
            other = jnp.where(inside, zero, other)
            for j in range(SUB):
                ratio = parts[j] * inverses[j]
                for i in range(j + 1, SUB):
                    parts[i] = parts[i] - ratio * across[j][i]
                other = other - ratio * pivot_rows[j]
            work_ref[g * SUB : (g + 1) * SUB, :] = other
        pivot_column = pivots[0]
        for j in range(1, SUB):
            pivot_column = jnp.where(place == j, pivots[j], pivot_column)
        root = jnp.sqrt(pivot_column)
        scale = 1.0 / root
        rows = rows * scale
        upper = jnp.where(lane >= first + SUB, rows, zero)
        for j in range(SUB):
            upper = jnp.where((lane == first + j) & (place <= j), columns[j] * scale, upper)
        upper_ref[at + first : at + first + SUB, at : at + HALF] = upper
        inverse_ref[at + first : at + first + SUB, at : at + HALF] = jnp.where(
            lane < first + SUB, rows, zero
        )


def factor_gram(top, side, end, work_ref, upper_ref, inverse_ref):
    work_ref[...] = top
    eliminate(work_ref, upper_ref, inverse_ref, 0)
    inverse_top = inverse_ref[0:HALF, 0:HALF]
    upper_side = mul(inverse_top, side, NN)
    upper_ref[0:HALF, HALF:] = upper_side
    upper_ref[HALF:, 0:HALF] = jnp.zeros((HALF, HALF), F32)
    work_ref[...] = end - mul(upper_side, upper_side, TN)
    carried = mul(upper_side, inverse_top, TN)
    eliminate(work_ref, upper_ref, inverse_ref, HALF)
    inverse_ref[HALF:, 0:HALF] = -mul(inverse_ref[HALF:, HALF:], carried, NN)
    inverse_ref[0:HALF, HALF:] = jnp.zeros((HALF, HALF), F32)


def two_sum(a, b):
    total = a + b
    other = total - a
    return total, (a - (total - other)) + (b - other)


def part(x, anchor):
    return (x + anchor) - anchor


def bf16_dot(a, b):
    return lax.dot_general(a, b, TN, preferred_element_type=F32)


def corners(shape):
    return (
        lax.broadcasted_iota(jnp.int32, shape, 0),
        lax.broadcasted_iota(jnp.int32, shape, 1),
    )


CHUNK = 256
PIECE = HALF + SUB
ANCHOR = 1.5 * 2.0**17
STEP = 2.0**-7


def pack(mine_ref, theirs_ref, at, square, low):
    row, column = corners((HALF, HALF))
    top, end = square[0:HALF, 0:HALF], square[HALF:, HALF:]
    diagonal = jnp.sum(jnp.where(row == column, end, 0.0), axis=0, keepdims=True)
    side = square[0:HALF, HALF:]
    mixed = jnp.where(row <= column, top, end)
    diagonal = jnp.broadcast_to(diagonal, (SUB, HALF))
    mine_ref[at : at + HALF, :] = jnp.where(low, side, mixed)
    theirs_ref[at : at + HALF, :] = jnp.where(low, mixed, side)
    mine_ref[at + HALF : at + PIECE, :] = diagonal
    theirs_ref[at + HALF : at + PIECE, :] = diagonal


def unpack(mine_ref, theirs_ref, at, low):
    row, column = corners((HALF, HALF))
    mine, theirs = mine_ref[at : at + HALF, :], theirs_ref[at : at + HALF, :]
    side = jnp.where(low, mine, theirs)
    mixed = jnp.where(low, theirs, mine)
    edge = slice(at + HALF, at + HALF + 1)
    diagonal = jnp.where(low, mine_ref[edge, :], theirs_ref[edge, :])
    turned = mixed.T
    top = jnp.where(row <= column, mixed, turned)
    end = jnp.where(row > column, mixed, jnp.where(row < column, turned, diagonal))
    return top, side, end


def gram_kernel(core_ref, mine_ref, theirs_ref, exact_ref, cross_ref, rest_ref, missing_ref):
    largest = jnp.max(jnp.abs(core_ref[...].astype(jnp.bfloat16).astype(F32)), axis=0, keepdims=True)
    anchor = jnp.broadcast_to(largest * ANCHOR, (CHUNK, core_ref.shape[1]))
    exact_ref[...] = jnp.zeros_like(exact_ref)
    cross_ref[...] = jnp.zeros_like(cross_ref)
    rest_ref[...] = jnp.zeros_like(rest_ref)
    missing_ref[...] = jnp.zeros_like(missing_ref)

    @pl.loop(0, core_ref.shape[0] // CHUNK)
    def _(step):
        core = core_ref[pl.ds(pl.multiple_of(step * CHUNK, CHUNK), CHUNK), :]
        halved = core.astype(jnp.bfloat16)
        wide = halved.astype(F32)
        missing = core - wide
        missing_high = missing.astype(jnp.bfloat16)
        missing_wide = missing_high.astype(F32)
        low_wide = missing - missing_wide
        missing_low = low_wide.astype(jnp.bfloat16)
        half_low = (0.5 * low_wide).astype(jnp.bfloat16)
        half_missing = (0.5 * missing_wide).astype(jnp.bfloat16)
        a = part(wide, anchor)
        left = wide - a
        b = part(left, anchor * STEP)
        c = left - b
        low = lambda x: x.astype(jnp.bfloat16)
        a16, b16, c16 = low(a), low(b), low(c)
        half_b, half_c = low(0.5 * b), low(0.5 * c)
        exact_ref[...] += bf16_dot(a16, a16)
        cross_ref[...] += bf16_dot(a16, b16)
        rest_ref[...] += bf16_dot(
            jnp.concatenate([a16, b16, b16, half_c], axis=0),
            jnp.concatenate([c16, half_b, c16, c16], axis=0),
        )
        missing_ref[...] += bf16_dot(
            jnp.concatenate([halved, halved, half_missing, missing_high, half_low], axis=0),
            jnp.concatenate([missing_high, missing_low, missing_high, missing_low, missing_low], axis=0),
        )

    cross, rest, missing = cross_ref[...], rest_ref[...], missing_ref[...]
    high, first = two_sum(exact_ref[...], cross)
    high, second = two_sum(high, cross.T)
    high, third = two_sum(high, rest + rest.T)
    low_core = lax.axis_index("qb") == 0
    pack(mine_ref, theirs_ref, 0, high, low_core)
    pack(mine_ref, theirs_ref, PIECE, ((first + second) + third) + (missing + missing.T), low_core)


def piece_order(place, rank, own_rows):
    depth = 4
    long = rank // (depth * own_rows)
    source, at = corners((rank, rank))
    quarter, z, row = at // (long * own_rows), at // own_rows % long, at % own_rows
    z = (z & 1) * 4 + (z & 2) + (z >> 2)
    shift = jnp.where(quarter == 1, depth - 1, jnp.where(quarter == 2, 1, jnp.where(quarter == 3, 2, 0)))
    y = (place + shift) & (depth - 1)
    return jnp.where(source == (z * depth + y) * own_rows + row, 1.0, 0.0)


def basis_kernel(scale, mine_ref, theirs_ref, core_ref, ortho_ref, factor_ref, work_ref, upper_ref, inverse_ref, lack_ref, other_ref, second_ref):
    low_core = lax.axis_index("qb") == 0
    top, side, end = (x * scale for x in unpack(mine_ref, theirs_ref, 0, low_core))
    lack_ref[0:HALF, 0:HALF] = top
    lack_ref[0:HALF, HALF:] = side
    lack_ref[HALF:, 0:HALF] = side.T
    lack_ref[HALF:, HALF:] = end
    factor_gram(top, side, end, work_ref, upper_ref, inverse_ref)

    upper = upper_ref[...]
    anchor = jnp.broadcast_to(jnp.max(jnp.abs(upper), axis=0, keepdims=True) * ANCHOR, upper.shape)
    low = lambda x: x.astype(jnp.bfloat16)
    a = part(upper, anchor)
    left = upper - a
    b = part(left, anchor * STEP)
    left = left - b
    c = part(left, anchor * (STEP * STEP))
    d = left - c
    a16, b16, c16, d16 = low(a), low(b), low(c), low(d)
    half_b, half_c = low(0.5 * b), low(0.5 * c)
    exact = bf16_dot(a16, a16)
    cross = bf16_dot(a16, b16)
    rest = bf16_dot(
        jnp.concatenate([a16, b16, a16, b16, b16, c16, c16], axis=0),
        jnp.concatenate([c16, half_b, d16, c16, d16, half_c, d16], axis=0),
    )
    left, first = two_sum(lack_ref[...], -exact)
    left, second = two_sum(left, -cross)
    left, third = two_sum(left, -cross.T)
    lack_ref[...] = left + (((first + second) + third) - (rest + rest.T))
    top, side, end = (x * scale for x in unpack(mine_ref, theirs_ref, PIECE, low_core))
    lack_ref[0:HALF, 0:HALF] += top
    lack_ref[0:HALF, HALF:] += side
    lack_ref[HALF:, 0:HALF] += side.T
    lack_ref[HALF:, HALF:] += end

    other_ref[...] = mul(mul(inverse_ref[...], lack_ref[...], NN), inverse_ref[...], NT)
    row, column = corners((HALF, HALF))
    unit = jnp.where(row == column, 1.0, 0.0)
    factor_gram(
        unit + other_ref[0:HALF, 0:HALF],
        other_ref[0:HALF, HALF:],
        unit + other_ref[HALF:, HALF:],
        work_ref,
        second_ref,
        lack_ref,
    )
    at = lax.axis_index("wide")
    mine = second_ref[pl.ds(pl.multiple_of(at * SUB, SUB), SUB), :]
    order = piece_order(at, core_ref.shape[1], factor_ref.shape[0])
    factor_ref[...] = mul(mul(mine, upper_ref[...], NN), order, NN)
    other_ref[...] = mul(lack_ref[...], inverse_ref[...], NN)

    @pl.loop(0, core_ref.shape[0] // CHUNK)
    def _(step):
        here = pl.ds(pl.multiple_of(step * CHUNK, CHUNK), CHUNK)
        ortho_ref[here, :] = mul(core_ref[here, :], other_ref[...], NT)


def next_kernel(factor_ref, own_ref, right_ref, left_ref, far_ref, out_ref):
    low = lambda x: x.astype(jnp.bfloat16)
    factor = factor_ref[...]
    first = low(factor)
    left = factor - first.astype(F32)
    second = low(left)
    third = low(left - second.astype(F32))
    stacked = jnp.concatenate([first.astype(F32), second.astype(F32), third.astype(F32)], axis=0)
    stacked = low(stacked)
    wide = 256

    for step in range(out_ref.shape[1] // wide):
        here = slice(step * wide, (step + 1) * wide)
        pieces = (own_ref, right_ref, left_ref, far_ref)
        values = jnp.concatenate([piece[:, here] for piece in pieces], axis=0)
        high = low(values)
        rest = low(values - high.astype(F32))
        dot = lambda b: lax.dot_general(stacked, b, NN, preferred_element_type=F32)
        whole = dot(high) + dot(rest)
        out_ref[:, here] = whole[0:SUB] + (whole[SUB : 2 * SUB] + whole[2 * SUB :])


def make_calls(rows, rank, scale, own_rows=SUB):
    tall = jax.ShapeDtypeStruct((rows, rank), F32)
    packed = jax.ShapeDtypeStruct((2 * PIECE, HALF), F32)
    vmem = pl.BlockSpec(memory_space=pltpu.VMEM)
    whole = pltpu.VMEM((rank, rank), F32)
    cost = pl.CostEstimate(
        flops=20 * rows * rank * rank, bytes_accessed=8 * rows * rank, transcendentals=0
    )
    gram = pl.pallas_call(
        gram_kernel,
        out_shape=(packed, packed),
        in_specs=[vmem],
        out_specs=(vmem, vmem),
        scratch_shapes=[whole] * 4,
        cost_estimate=cost,
    )
    basis = pl.pallas_call(
        functools.partial(basis_kernel, scale),
        out_shape=(tall, jax.ShapeDtypeStruct((own_rows, rank), F32)),
        in_specs=[vmem] * 3,
        out_specs=(vmem,) * 2,
        scratch_shapes=[pltpu.VMEM((HALF, HALF), F32)] + [whole] * 5,
        cost_estimate=cost,
    )
    return gram, basis


def shifted(value, pairs):
    return lax.ppermute(value, ("wide", "qa", "qb"), pairs)


def add_pairs(x, y):
    high, lost = two_sum(x[:PIECE], y[:PIECE])
    return jnp.concatenate([high, (x[PIECE:] + y[PIECE:]) + lost], axis=0)


def tie(*values):
    return lax.optimization_barrier(values)


def sum_and_spread(gram, core_slices, next_core):
    depth = 4
    wide, across, cores = (lax.axis_size(n) for n in ("wide", "qa", "qb"))
    long = wide // depth
    z_bits = lax.axis_index("wide") // depth

    def pairs(source):
        out = []
        for i in range(wide * across * cores):
            z, y, x, core = i // (cores * across * depth), i // (cores * across) % depth, i // cores % across, i % cores
            z2, y2, x2, core2 = source(z, y, x, core)
            out.append(((((z2 % long) * depth + y2 % depth) * across + x2 % across) * cores + core2 % cores, i))
        return out

    def around(value, source):
        one, two, three = (shifted(value, pairs(functools.partial(source, d))) for d in (1, 2, -1))
        return add_pairs(add_pairs(value, two), add_pairs(one, three))

    def partner(value, bit):
        return shifted(value, pairs(lambda z, y, x, core: (z ^ bit, y, x, core)))

    def merge(own, other, bit):
        first = (z_bits & bit) == 0
        return jnp.concatenate([jnp.where(first, own, other), jnp.where(first, other, own)], axis=0)

    def beside(value, d):
        return shifted(value, pairs(lambda z, y, x, core: (z, y + d, x, core)))

    swap = pairs(lambda z, y, x, core: (z, y, x, 1 - core))
    other = partner(next_core, 4)
    mine, theirs = gram(core_slices)
    mine = add_pairs(mine, shifted(theirs, swap))
    mine, other = tie(mine, other)
    rows = merge(next_core, other, 4)
    other = partner(rows, 2)
    mine = around(mine, lambda d, z, y, x, core: (z, y, x + d, core) if core == 0 else (z, y + d, x, core))
    mine, other = tie(mine, other)
    rows = merge(rows, other, 2)
    other = partner(rows, 1)
    mine = around(mine, lambda d, z, y, x, core: (z, y, x + d, core) if core == 1 else (z, y + d, x, core))
    mine, other = tie(mine, other)
    rows = merge(rows, other, 1)
    right = beside(rows, -1)
    left = beside(rows, 1)
    far = beside(rows, 2)
    other = shifted(mine, pairs(lambda z, y, x, core: (z + 4, y, x, core)))
    mine = add_pairs(mine, other)
    mine = around(mine, lambda d, z, y, x, core: (z + d, y, x, core))
    theirs = shifted(mine, swap)
    mine, theirs, right, left = tie(mine, theirs, right, left)
    return (mine, theirs), (rows, right, left, far)


def per_device(core_slices, next_core):
    rows, rank = core_slices.shape
    own_rows = next_core.shape[0]
    total_rows = rows * lax.axis_size("wide") * lax.axis_size("qa") * lax.axis_size("qb")
    gram, basis = make_calls(rows, rank, 1.0 / total_rows, own_rows)
    vmem = pl.BlockSpec(memory_space=pltpu.VMEM)
    total, pieces = sum_and_spread(gram, core_slices, next_core)
    ortho_basis, factor = basis(*total, core_slices)
    new_core = pl.pallas_call(
        next_kernel,
        out_shape=jax.ShapeDtypeStruct(next_core.shape, F32),
        in_specs=[vmem] * 5,
        out_specs=vmem,
    )(factor, *pieces)
    return (ortho_basis, new_core)


def solution(mesh):
    return jax.shard_map(
        per_device,
        mesh=mesh,
        in_specs=(P(("wide", "qa", "qb"), None), P("wide", ("qa", "qb"))),
        out_specs=(P(("wide", "qa", "qb"), None), P("wide", ("qa", "qb"))),
        check_vma=False,
    )
```

```python
import functools

import jax
import jax.numpy as jnp
from jax import lax
from jax.experimental import pallas as pl
from jax.experimental.pallas import tpu as pltpu
from jax.sharding import PartitionSpec as P


HALF = 128
SUB = 8
F32 = jnp.float32
NT = (((1,), (1,)), ((), ()))
NN = (((1,), (0,)), ((), ()))
TN = (((0,), (0,)), ((), ()))


def mul(a, b, dims):
    return lax.dot_general(
        a, b, dims, precision=lax.Precision.HIGHEST, preferred_element_type=F32
    )


def row_of(x, j):
    return jnp.broadcast_to(x[j : j + 1, :], x.shape)


def column_of(x, k):
    return jnp.broadcast_to(x[:, k : k + 1], x.shape)


def eliminate(work_ref, upper_ref, inverse_ref, at):
    groups = HALF // SUB
    lane = lax.broadcasted_iota(jnp.int32, (SUB, HALF), 1)
    place = lax.broadcasted_iota(jnp.int32, (SUB, HALF), 0)
    zero = jnp.zeros((SUB, HALF), F32)
    for b in range(groups):
        first = b * SUB
        inside = (lane >= first) & (lane < first + SUB)
        own = work_ref[first : first + SUB, :]
        columns = [column_of(own, first + j) for j in range(SUB)]
        rows = jnp.where(inside, jnp.where(lane - first == place, 1.0, 0.0), own)
        inverses, across, pivots, pivot_rows = [], [], [], []
        for j in range(SUB):
            pivot = row_of(columns[j], j)
            inverse = 1.0 / pivot
            ratio = jnp.where(place > j, columns[j] * inverse, zero)
            ahead = {}
            for i in range(j + 1, SUB):
                ahead[i] = row_of(columns[i], j)
                columns[i] = columns[i] - ratio * ahead[i]
            pivot_row = row_of(rows, j)
            rows = rows - ratio * pivot_row
            inverses.append(inverse)
            across.append(ahead)
            pivots.append(pivot)
            pivot_rows.append(pivot_row)
        for g in range(b + 1, groups):
            other = work_ref[g * SUB : (g + 1) * SUB, :]
            parts = [column_of(other, first + j) for j in range(SUB)]
            other = jnp.where(inside, zero, other)
            for j in range(SUB):
                ratio = parts[j] * inverses[j]
                for i in range(j + 1, SUB):
                    parts[i] = parts[i] - ratio * across[j][i]
                other = other - ratio * pivot_rows[j]
            work_ref[g * SUB : (g + 1) * SUB, :] = other
        pivot_column = pivots[0]
        for j in range(1, SUB):
            pivot_column = jnp.where(place == j, pivots[j], pivot_column)
        root = jnp.sqrt(pivot_column)
        scale = 1.0 / root
        rows = rows * scale
        upper = jnp.where(lane >= first + SUB, rows, zero)
        for j in range(SUB):
            upper = jnp.where((lane == first + j) & (place <= j), columns[j] * scale, upper)
        upper_ref[at + first : at + first + SUB, at : at + HALF] = upper
        inverse_ref[at + first : at + first + SUB, at : at + HALF] = jnp.where(
            lane < first + SUB, rows, zero
        )


def factor_gram(top, side, end, work_ref, upper_ref, inverse_ref):
    work_ref[...] = top
    eliminate(work_ref, upper_ref, inverse_ref, 0)
    inverse_top = inverse_ref[0:HALF, 0:HALF]
    upper_side = mul(inverse_top, side, NN)
    upper_ref[0:HALF, HALF:] = upper_side
    upper_ref[HALF:, 0:HALF] = jnp.zeros((HALF, HALF), F32)
    work_ref[...] = end - mul(upper_side, upper_side, TN)
    carried = mul(upper_side, inverse_top, TN)
    eliminate(work_ref, upper_ref, inverse_ref, HALF)
    inverse_ref[HALF:, 0:HALF] = -mul(inverse_ref[HALF:, HALF:], carried, NN)
    inverse_ref[0:HALF, HALF:] = jnp.zeros((HALF, HALF), F32)


def two_sum(a, b):
    total = a + b
    other = total - a
    return total, (a - (total - other)) + (b - other)


def part(x, anchor):
    return (x + anchor) - anchor


def bf16_dot(a, b):
    return lax.dot_general(a, b, TN, preferred_element_type=F32)


def corners(shape):
    return (
        lax.broadcasted_iota(jnp.int32, shape, 0),
        lax.broadcasted_iota(jnp.int32, shape, 1),
    )


CHUNK = 256
PIECE = HALF + SUB
ANCHOR = 1.5 * 2.0**17
STEP = 2.0**-7


def pack(mine_ref, theirs_ref, at, square, low):
    row, column = corners((HALF, HALF))
    top, end = square[0:HALF, 0:HALF], square[HALF:, HALF:]
    diagonal = jnp.sum(jnp.where(row == column, end, 0.0), axis=0, keepdims=True)
    side = square[0:HALF, HALF:]
    mixed = jnp.where(row <= column, top, end)
    diagonal = jnp.broadcast_to(diagonal, (SUB, HALF))
    mine_ref[at : at + HALF, :] = jnp.where(low, side, mixed)
    theirs_ref[at : at + HALF, :] = jnp.where(low, mixed, side)
    mine_ref[at + HALF : at + PIECE, :] = diagonal
    theirs_ref[at + HALF : at + PIECE, :] = diagonal


def unpack(mine_ref, theirs_ref, at, low):
    row, column = corners((HALF, HALF))
    mine, theirs = mine_ref[at : at + HALF, :], theirs_ref[at : at + HALF, :]
    side = jnp.where(low, mine, theirs)
    mixed = jnp.where(low, theirs, mine)
    edge = slice(at + HALF, at + HALF + 1)
    diagonal = jnp.where(low, mine_ref[edge, :], theirs_ref[edge, :])
    turned = mixed.T
    top = jnp.where(row <= column, mixed, turned)
    end = jnp.where(row > column, mixed, jnp.where(row < column, turned, diagonal))
    return top, side, end


def gram_kernel(core_ref, mine_ref, theirs_ref, exact_ref, cross_ref, rest_ref, missing_ref):
    largest = jnp.max(jnp.abs(core_ref[...].astype(jnp.bfloat16).astype(F32)), axis=0, keepdims=True)
    anchor = jnp.broadcast_to(largest * ANCHOR, (CHUNK, core_ref.shape[1]))
    exact_ref[...] = jnp.zeros_like(exact_ref)
    cross_ref[...] = jnp.zeros_like(cross_ref)
    rest_ref[...] = jnp.zeros_like(rest_ref)
    missing_ref[...] = jnp.zeros_like(missing_ref)

    @pl.loop(0, core_ref.shape[0] // CHUNK)
    def _(step):
        core = core_ref[pl.ds(pl.multiple_of(step * CHUNK, CHUNK), CHUNK), :]
        halved = core.astype(jnp.bfloat16)
        wide = halved.astype(F32)
        missing = core - wide
        missing_high = missing.astype(jnp.bfloat16)
        missing_wide = missing_high.astype(F32)
        low_wide = missing - missing_wide
        missing_low = low_wide.astype(jnp.bfloat16)
        half_low = (0.5 * low_wide).astype(jnp.bfloat16)
        half_missing = (0.5 * missing_wide).astype(jnp.bfloat16)
        a = part(wide, anchor)
        left = wide - a
        b = part(left, anchor * STEP)
        c = left - b
        low = lambda x: x.astype(jnp.bfloat16)
        a16, b16, c16 = low(a), low(b), low(c)
        half_b, half_c = low(0.5 * b), low(0.5 * c)
        exact_ref[...] += bf16_dot(a16, a16)
        cross_ref[...] += bf16_dot(a16, b16)
        rest_ref[...] += bf16_dot(
            jnp.concatenate([a16, b16, b16, half_c], axis=0),
            jnp.concatenate([c16, half_b, c16, c16], axis=0),
        )
        missing_ref[...] += bf16_dot(
            jnp.concatenate([halved, halved, half_missing, missing_high, half_low], axis=0),
            jnp.concatenate([missing_high, missing_low, missing_high, missing_low, missing_low], axis=0),
        )

    cross, rest, missing = cross_ref[...], rest_ref[...], missing_ref[...]
    high, first = two_sum(exact_ref[...], cross)
    high, second = two_sum(high, cross.T)
    high, third = two_sum(high, rest + rest.T)
    low_core = lax.axis_index("qb") == 0
    pack(mine_ref, theirs_ref, 0, high, low_core)
    pack(mine_ref, theirs_ref, PIECE, ((first + second) + third) + (missing + missing.T), low_core)


def piece_order(place, rank, own_rows):
    depth = 4
    long = rank // (depth * own_rows)
    source, at = corners((rank, rank))
    quarter, z, row = at // (long * own_rows), at // own_rows % long, at % own_rows
    z = (z & 1) * 4 + (z & 2) + (z >> 2)
    shift = jnp.where(quarter == 1, depth - 1, jnp.where(quarter == 2, 1, jnp.where(quarter == 3, 2, 0)))
    y = (place + shift) & (depth - 1)
    return jnp.where(source == (z * depth + y) * own_rows + row, 1.0, 0.0)


def basis_kernel(scale, mine_ref, theirs_ref, core_ref, ortho_ref, factor_ref, work_ref, upper_ref, inverse_ref, lack_ref, other_ref, second_ref):
    low_core = lax.axis_index("qb") == 0
    top, side, end = (x * scale for x in unpack(mine_ref, theirs_ref, 0, low_core))
    lack_ref[0:HALF, 0:HALF] = top
    lack_ref[0:HALF, HALF:] = side
    lack_ref[HALF:, 0:HALF] = side.T
    lack_ref[HALF:, HALF:] = end
    factor_gram(top, side, end, work_ref, upper_ref, inverse_ref)

    upper = upper_ref[...]
    anchor = jnp.broadcast_to(jnp.max(jnp.abs(upper), axis=0, keepdims=True) * ANCHOR, upper.shape)
    low = lambda x: x.astype(jnp.bfloat16)
    a = part(upper, anchor)
    left = upper - a
    b = part(left, anchor * STEP)
    left = left - b
    c = part(left, anchor * (STEP * STEP))
    d = left - c
    a16, b16, c16, d16 = low(a), low(b), low(c), low(d)
    half_b, half_c = low(0.5 * b), low(0.5 * c)
    exact = bf16_dot(a16, a16)
    cross = bf16_dot(a16, b16)
    rest = bf16_dot(
        jnp.concatenate([a16, b16, a16, b16, b16, c16, c16], axis=0),
        jnp.concatenate([c16, half_b, d16, c16, d16, half_c, d16], axis=0),
    )
    left, first = two_sum(lack_ref[...], -exact)
    left, second = two_sum(left, -cross)
    left, third = two_sum(left, -cross.T)
    lack_ref[...] = left + (((first + second) + third) - (rest + rest.T))
    top, side, end = (x * scale for x in unpack(mine_ref, theirs_ref, PIECE, low_core))
    lack_ref[0:HALF, 0:HALF] += top
    lack_ref[0:HALF, HALF:] += side
    lack_ref[HALF:, 0:HALF] += side.T
    lack_ref[HALF:, HALF:] += end

    other_ref[...] = mul(mul(inverse_ref[...], lack_ref[...], NN), inverse_ref[...], NT)
    row, column = corners((HALF, HALF))
    unit = jnp.where(row == column, 1.0, 0.0)
    factor_gram(
        unit + other_ref[0:HALF, 0:HALF],
        other_ref[0:HALF, HALF:],
        unit + other_ref[HALF:, HALF:],
        work_ref,
        second_ref,
        lack_ref,
    )
    at = lax.axis_index("wide")
    mine = second_ref[pl.ds(pl.multiple_of(at * SUB, SUB), SUB), :]
    order = piece_order(at, core_ref.shape[1], factor_ref.shape[0])
    factor_ref[...] = mul(mul(mine, upper_ref[...], NN), order, NN)
    other_ref[...] = mul(lack_ref[...], inverse_ref[...], NN)

    @pl.loop(0, core_ref.shape[0] // CHUNK)
    def _(step):
        here = pl.ds(pl.multiple_of(step * CHUNK, CHUNK), CHUNK)
        ortho_ref[here, :] = mul(core_ref[here, :], other_ref[...], NT)


def next_kernel(factor_ref, own_ref, right_ref, left_ref, far_ref, out_ref):
    low = lambda x: x.astype(jnp.bfloat16)
    factor = factor_ref[...]
    first = low(factor)
    left = factor - first.astype(F32)
    second = low(left)
    third = low(left - second.astype(F32))
    stacked = jnp.concatenate([first.astype(F32), second.astype(F32), third.astype(F32)], axis=0)
    stacked = low(stacked)
    wide = 256

    for step in range(out_ref.shape[1] // wide):
        here = slice(step * wide, (step + 1) * wide)
        pieces = (own_ref, right_ref, left_ref, far_ref)
        values = jnp.concatenate([piece[:, here] for piece in pieces], axis=0)
        high = low(values)
        rest = low(values - high.astype(F32))
        dot = lambda b: lax.dot_general(stacked, b, NN, preferred_element_type=F32)
        whole = dot(high) + dot(rest)
        out_ref[:, here] = whole[0:SUB] + (whole[SUB : 2 * SUB] + whole[2 * SUB :])


def make_calls(rows, rank, scale, own_rows=SUB):
    tall = jax.ShapeDtypeStruct((rows, rank), F32)
    packed = jax.ShapeDtypeStruct((2 * PIECE, HALF), F32)
    vmem = pl.BlockSpec(memory_space=pltpu.VMEM)
    whole = pltpu.VMEM((rank, rank), F32)
    cost = pl.CostEstimate(
        flops=20 * rows * rank * rank, bytes_accessed=8 * rows * rank, transcendentals=0
    )
    gram = pl.pallas_call(
        gram_kernel,
        out_shape=(packed, packed),
        in_specs=[vmem],
        out_specs=(vmem, vmem),
        scratch_shapes=[whole] * 4,
        cost_estimate=cost,
    )
    basis = pl.pallas_call(
        functools.partial(basis_kernel, scale),
        out_shape=(tall, jax.ShapeDtypeStruct((own_rows, rank), F32)),
        in_specs=[vmem] * 3,
        out_specs=(vmem,) * 2,
        scratch_shapes=[pltpu.VMEM((HALF, HALF), F32)] + [whole] * 5,
        cost_estimate=cost,
    )
    return gram, basis


def shifted(value, pairs):
    return lax.ppermute(value, ("wide", "qa", "qb"), pairs)


def add_pairs(x, y):
    high, lost = two_sum(x[:PIECE], y[:PIECE])
    return jnp.concatenate([high, (x[PIECE:] + y[PIECE:]) + lost], axis=0)


def tie(*values):
    return lax.optimization_barrier(values)


def sum_and_spread(gram, core_slices, next_core):
    depth = 4
    wide, across, cores = (lax.axis_size(n) for n in ("wide", "qa", "qb"))
    long = wide // depth
    z_bits = lax.axis_index("wide") // depth

    def pairs(source):
        out = []
        for i in range(wide * across * cores):
            z, y, x, core = i // (cores * across * depth), i // (cores * across) % depth, i // cores % across, i % cores
            z2, y2, x2, core2 = source(z, y, x, core)
            out.append(((((z2 % long) * depth + y2 % depth) * across + x2 % across) * cores + core2 % cores, i))
        return out

    def around(value, source):
        one, two, three = (shifted(value, pairs(functools.partial(source, d))) for d in (1, 2, -1))
        return add_pairs(add_pairs(value, two), add_pairs(one, three))

    def partner(value, bit):
        return shifted(value, pairs(lambda z, y, x, core: (z ^ bit, y, x, core)))

    def merge(own, other, bit):
        first = (z_bits & bit) == 0
        return jnp.concatenate([jnp.where(first, own, other), jnp.where(first, other, own)], axis=0)

    def beside(value, d):
        return shifted(value, pairs(lambda z, y, x, core: (z, y + d, x, core)))

    swap = pairs(lambda z, y, x, core: (z, y, x, 1 - core))
    other = partner(next_core, 4)
    mine, theirs = gram(core_slices)
    theirs = shifted(theirs, swap)
    rows = merge(next_core, other, 4)
    other = partner(rows, 2)
    mine = add_pairs(mine, theirs)
    mine = around(mine, lambda d, z, y, x, core: (z, y, x + d, core) if core == 0 else (z, y + d, x, core))
    mine, other = tie(mine, other)
    rows = merge(rows, other, 2)
    other = partner(rows, 1)
    mine = around(mine, lambda d, z, y, x, core: (z, y, x + d, core) if core == 1 else (z, y + d, x, core))
    mine, other = tie(mine, other)
    rows = merge(rows, other, 1)
    mine, rows = tie(mine, rows)
    right = beside(rows, -1)
    left = beside(rows, 1)
    far = beside(rows, 2)
    other = shifted(mine, pairs(lambda z, y, x, core: (z + 4, y, x, core)))
    mine = add_pairs(mine, other)
    mine = around(mine, lambda d, z, y, x, core: (z + d, y, x, core))
    theirs = shifted(mine, swap)
    mine, theirs, right, left = tie(mine, theirs, right, left)
    return (mine, theirs), (rows, right, left, far)


def per_device(core_slices, next_core):
    rows, rank = core_slices.shape
    own_rows = next_core.shape[0]
    total_rows = rows * lax.axis_size("wide") * lax.axis_size("qa") * lax.axis_size("qb")
    gram, basis = make_calls(rows, rank, 1.0 / total_rows, own_rows)
    vmem = pl.BlockSpec(memory_space=pltpu.VMEM)
    total, pieces = sum_and_spread(gram, core_slices, next_core)
    ortho_basis, factor = basis(*total, core_slices)
    new_core = pl.pallas_call(
        next_kernel,
        out_shape=jax.ShapeDtypeStruct(next_core.shape, F32),
        in_specs=[vmem] * 5,
        out_specs=vmem,
    )(factor, *pieces)
    return (ortho_basis, new_core)


def solution(mesh):
    return jax.shard_map(
        per_device,
        mesh=mesh,
        in_specs=(P(("wide", "qa", "qb"), None), P("wide", ("qa", "qb"))),
        out_specs=(P(("wide", "qa", "qb"), None), P("wide", ("qa", "qb"))),
        check_vma=False,
    )
```
